128 devices in a mesh: tok: 8 (over y, core), exp: 16 (over x, z).
Axes of the slice: x: 4, y: 4, z: 4, core: 2. Of those that a mesh axis runs over, the one named last changes fastest.
Arguments:
- tokens: bfloat16 [8192, 4096], P(('tok', 'exp')), may hold values from -6 to 6
- cotangent: bfloat16 [8192, 4096], P(('tok', 'exp')), may hold values from -6 to 6
- expert_ids: int32 [8192, 8], P(('tok', 'exp')), may hold values from 0 to 127, as said below
- gate_weights: bfloat16 [8192, 8], P(('tok', 'exp')), may hold values from 0.099609375 to 1
- w_in: bfloat16 [16, 2, 1536, 4096], P('exp', None, 'tok'), may hold values from -0.09375 to 0.09375
- w_down: bfloat16 [16, 1536, 4096], P('exp', 'tok'), may hold values from -0.3125 to 0.3125
Outputs:
- moe_out: bfloat16 [8192, 4096], P(('tok', 'exp'))
- token_grad: bfloat16 [8192, 4096], P(('tok', 'exp'))
- grad_w_in: bfloat16 [16, 2, 1536, 4096], P('exp', None, 'tok')
- grad_w_down: bfloat16 [16, 1536, 4096], P('exp', 'tok')
The draws below stay inside these ranges and needn't reach their ends.
Inputs may be any that keep to these rules, and one draw needn't show every extreme that they name: `expert_ids`: each row names 8 different experts. Among the 64 rows of one device no expert below 16 is named by more than 2 rows, and one expert below 16, the same on every device, is named by exactly 2 rows of every device.
All inputs are finite; a program needn't handle non-finite values.
Results may differ from the reference program's by a relative error of at most 0.0058.
Values may be sent and summed in bfloat16 or wider, within the bound.
A program may use at most 128 MiB of HBM per device.

```python
import math
import jax
import jax.numpy as jnp
from jax import lax

D = 4096
FF = 1536
EXPERTS_ALL = 128
TOP = 8
TOKENS_PER_CARD = 64
CAP = 2
EXPERTS = 16
TOKENS = 8192


def draw_expert_ids(key, part):
    blocks = TOKENS // TOKENS_PER_CARD
    hot_expert = jax.random.randint(jax.random.fold_in(key, 7), (), 0, EXPERTS).astype(jnp.int32)
    owners = jnp.arange(EXPERTS, dtype=jnp.int32)

    def one_block(block_row):
        block_key = jax.random.fold_in(jax.random.fold_in(key, 11), block_row)
        counts = jax.random.randint(jax.random.fold_in(block_key, 1), (EXPERTS,), 0, CAP + 1).astype(jnp.int32)
        counts = jnp.where(owners == hot_expert, CAP, counts).astype(jnp.int32)
        ranking = jax.random.permutation(jax.random.fold_in(block_key, 2), EXPERTS).astype(jnp.int32)
        row_order = jax.random.permutation(jax.random.fold_in(block_key, 3), TOKENS_PER_CARD).astype(jnp.int32)
        position = jnp.arange(EXPERTS * CAP, dtype=jnp.int32)
        expert_lookup = ranking[position // CAP]
        active_mask = position % CAP < counts[expert_lookup]
        row_lookup = row_order[position]
        pending_rows = jnp.full((TOKENS_PER_CARD,), -1, jnp.int32).at[row_lookup].set(jnp.where(active_mask, expert_lookup, -1).astype(jnp.int32))
        outside = jnp.arange(EXPERTS, EXPERTS_ALL, dtype=jnp.int32)
        table = jnp.broadcast_to(outside[None, :], (TOKENS_PER_CARD, EXPERTS_ALL - EXPERTS))
        remaining_peers = jax.random.permutation(jax.random.fold_in(block_key, 4), table, axis=1, independent=True)[:, :TOP]
        column_slot = jax.random.randint(jax.random.fold_in(block_key, 5), (TOKENS_PER_CARD,), 0, TOP).astype(jnp.int32)
        place_table = jnp.arange(TOP, dtype=jnp.int32)
        substitute_rows = (place_table[None, :] == column_slot[:, None]) & (pending_rows[:, None] >= 0)
        return jnp.where(substitute_rows, pending_rows[:, None], remaining_peers).astype(jnp.int32)
    picks_all = jax.vmap(one_block)(jnp.arange(blocks, dtype=jnp.int32))
    return picks_all.reshape(TOKENS, TOP).astype(jnp.int32)


def block_scale(rng, shape, cuts, low, top_value):
    def one(dim, parts):
        heights = jax.random.uniform(jax.random.fold_in(jax.random.fold_in(rng, 6), dim), (parts,), jnp.float32, low / len(cuts), top_value / len(cuts))
        return jnp.repeat(jnp.exp(heights), shape[dim] // parts).reshape((-1,) + (1,) * (len(shape) - dim - 1))

    gain = one(*cuts[0])
    for cut in cuts[1:]:
        gain = gain * one(*cut)
    return gain


def normal_values(key, shape, deviation, most, split=(), held_as=jnp.bfloat16):
    array = deviation * jax.random.normal(key, shape, jnp.float32)
    if split:
        array = array * block_scale(key, shape, split, -0.22, 0.18)
    return jnp.clip(array, -most, most).astype(held_as)


def setup_inputs(seed: int = 0) -> dict:
    keys = jax.random.split(jax.random.key(seed), 7)
    return {
        "tokens": normal_values(keys[0], (TOKENS, D), 1.0, 6.0, ((0, 128),)),
        "cotangent": normal_values(keys[1], (TOKENS, D), 1.0, 6.0, ((0, 128),)),
        "expert_ids": draw_expert_ids(jax.random.fold_in(keys[6], 71), 0),
        "gate_weights": jnp.clip(jnp.exp(math.log(1.0) - 2.306499 * jax.random.uniform(keys[3], (TOKENS, TOP), jnp.float32) ** block_scale(keys[3], (TOKENS, TOP), ((0, 128),), -0.2, 0.2)), 0.099609375, 1.0).astype(jnp.bfloat16),
        "w_in": normal_values(keys[4], (EXPERTS, 2, FF, D), D ** -0.5, 0.09375, ((0, 16), (2, 8))),
        "w_down": normal_values(keys[5], (EXPERTS, FF, D), (FF // 4) ** -0.5, 0.3125, ((0, 16), (1, 8))),
    }


def expert_pass(operands):
    routed, routed_cot, weight_in, weight_down = operands
    gate_act = jnp.dot(routed, weight_in[0].T, preferred_element_type=jnp.float32)
    up_act = jnp.dot(routed, weight_in[1].T, preferred_element_type=jnp.float32)
    sigmoid_gate = jax.nn.sigmoid(gate_act)
    silu_gate = gate_act * sigmoid_gate
    hidden = (silu_gate * up_act).astype(jnp.bfloat16)
    expert_out = jnp.dot(hidden, weight_down, preferred_element_type=jnp.float32).astype(jnp.bfloat16)
    hidden_grad = jnp.dot(routed_cot, weight_down.T, preferred_element_type=jnp.float32)
    gate_grad = (hidden_grad * up_act * sigmoid_gate * (1.0 + gate_act * (1.0 - sigmoid_gate))).astype(jnp.bfloat16)
    up_grad = (hidden_grad * silu_gate).astype(jnp.bfloat16)
    input_grad = (jnp.dot(gate_grad, weight_in[0], preferred_element_type=jnp.float32)
                  + jnp.dot(up_grad, weight_in[1], preferred_element_type=jnp.float32)).astype(jnp.bfloat16)
    grad_gate = jnp.dot(gate_grad.T, routed, preferred_element_type=jnp.float32).astype(jnp.bfloat16)
    grad_up = jnp.dot(up_grad.T, routed, preferred_element_type=jnp.float32).astype(jnp.bfloat16)
    grad_down = jnp.dot(hidden.T, routed_cot, preferred_element_type=jnp.float32).astype(jnp.bfloat16)
    return expert_out, input_grad, jnp.stack([grad_gate, grad_up]), grad_down


def place_rows(expert_ids):
    blocks = TOKENS // TOKENS_PER_CARD
    flat_ids = expert_ids.reshape(blocks, TOKENS_PER_CARD * TOP).astype(jnp.int32)
    owners = jnp.arange(EXPERTS, dtype=jnp.int32)
    onehot = (flat_ids[:, :, None] == owners[None, None, :]).astype(jnp.int32)
    before = (jnp.cumsum(onehot, axis=1).astype(jnp.int32) - onehot).astype(jnp.int32)
    slots = jnp.sum(before * onehot, axis=2).astype(jnp.int32)
    block_row = jnp.arange(blocks, dtype=jnp.int32)[:, None]
    row_index = flat_ids * (blocks * CAP) + block_row * CAP + slots
    row_index = jnp.where(flat_ids < EXPERTS, row_index, EXPERTS * blocks * CAP).astype(jnp.int32)
    return row_index.reshape(TOKENS, TOP)


def reference(tokens, cotangent, expert_ids, gate_weights, w_in, w_down):
    blocks = TOKENS // TOKENS_PER_CARD
    rows_total = EXPERTS * blocks * CAP
    row_index = place_rows(expert_ids)
    flat_index = row_index.reshape(-1)
    token_of = jnp.broadcast_to(jnp.arange(TOKENS, dtype=jnp.int32)[:, None], (TOKENS, TOP)).reshape(-1)
    source = jnp.full((rows_total,), TOKENS, jnp.int32).at[flat_index].set(token_of, mode="drop")
    gate_rows = jnp.zeros((rows_total,), jnp.float32).at[flat_index].set(
        gate_weights.astype(jnp.float32).reshape(-1), mode="drop")
    padded_tokens = jnp.concatenate([tokens, jnp.zeros((1, D), tokens.dtype)], axis=0)
    padded_cot = jnp.concatenate([cotangent, jnp.zeros((1, D), cotangent.dtype)], axis=0)
    routed = padded_tokens[source]
    routed_cot = (gate_rows[:, None] * padded_cot[source].astype(jnp.float32)).astype(jnp.bfloat16)
    routed = routed.reshape(EXPERTS, blocks * CAP, D)
    routed_cot = routed_cot.reshape(EXPERTS, blocks * CAP, D)
    expert_out, input_grad, grad_w_in, grad_w_down = lax.map(expert_pass, (routed, routed_cot, w_in, w_down))
    out_pad = jnp.concatenate([expert_out.reshape(rows_total, D), jnp.zeros((1, D), jnp.bfloat16)], axis=0)
    grad_pad = jnp.concatenate([input_grad.reshape(rows_total, D), jnp.zeros((1, D), jnp.bfloat16)], axis=0)
    moe_sum = jnp.zeros((TOKENS, D), jnp.float32)
    grad_sum = jnp.zeros((TOKENS, D), jnp.float32)
    for place in range(TOP):
        picked = row_index[:, place]
        moe_sum = moe_sum + gate_weights[:, place].astype(jnp.float32)[:, None] * out_pad[picked].astype(jnp.float32)
        grad_sum = grad_sum + grad_pad[picked].astype(jnp.float32)
    return moe_sum.astype(jnp.bfloat16), grad_sum.astype(jnp.bfloat16), grad_w_in, grad_w_down
```

```python
import functools

import jax
import jax.numpy as jnp
from jax import lax
from jax.experimental import pallas as pl
from jax.experimental.pallas import tpu as pltpu
from jax.sharding import PartitionSpec as P

CAP = 2
PIECES = 8
BF16 = jnp.bfloat16
F32 = jnp.float32
MESH = pl.DeviceIdType.MESH


def dot(a, b):
    return jnp.dot(a, b, preferred_element_type=F32)


def dot_nt(a, b):
    return lax.dot_general(a, b, (((1,), (1,)), ((), ())), preferred_element_type=F32)


def dot_tn(a, b):
    return lax.dot_general(a, b, (((0,), (0,)), ((), ())), preferred_element_type=F32)


def iota(shape, dim):
    return lax.broadcasted_iota(jnp.int32, shape, dim)


def kernel(
    experts,
    ids_ref,
    gates_ref,
    tok_hbm,
    cot_hbm,
    win_hbm,
    wdn_hbm,
    moe_hbm,
    tgr_hbm,
    gin_hbm,
    gdn_hbm,
    src,
    win,
    wdn,
    slab,
    land,
    x,
    act,
    hid,
    part,
    mate,
    summed,
    far,
    near,
    gin,
    gdn,
    outs,
    in_sem,
    out_sem,
    own_sem,
    a2a_send,
    a2a_recv,
    ag_send,
    ag_recv,
    rs_send,
    rs_recv,
):
    rows, dim = tok_hbm.shape
    width = dim // PIECES
    ff = wdn_hbm.shape[1]
    group = CAP * PIECES
    slots = CAP * experts
    msg_rows = experts * group
    all_rows = 8 * slots

    t = lax.axis_index("tok")
    e = lax.axis_index("exp")
    up = lax.rem(t + 2, 8)
    opp = lax.rem(t + 4, 8)
    dn = lax.rem(t + 6, 8)
    mate_t = t + 1 - 2 * lax.rem(t, 2)

    barrier = pltpu.get_barrier_semaphore()
    for k in range(1, experts):
        pl.semaphore_signal(
            barrier, inc=1, device_id=(t, lax.rem(e + k, experts)), device_id_type=MESH
        )
    for other in (up, dn, mate_t):
        pl.semaphore_signal(barrier, inc=1, device_id=(other, e), device_id_type=MESH)

    loads = []
    for q, hbm in enumerate((tok_hbm, cot_hbm)):
        group_loads = []
        for j in range(PIECES):
            copy = pltpu.make_async_copy(
                hbm.at[:, pl.ds(j * width, width)],
                src.at[q, pl.ds(j * rows, rows)],
                in_sem.at[q * PIECES + j],
            )
            copy.start()
            group_loads.append(copy)
        loads.append(group_loads)
    load_win = pltpu.make_async_copy(win_hbm.at[0], win, in_sem.at[2 * PIECES])
    load_wdn = pltpu.make_async_copy(wdn_hbm.at[0], wdn, in_sem.at[2 * PIECES + 1])
    load_win.start()
    load_wdn.start()

    def remote(a, b, ssem, rsem, dev_t, dev_e):
        return pltpu.make_async_remote_copy(
            src_ref=a,
            dst_ref=b,
            send_sem=ssem,
            recv_sem=rsem,
            device_id=(dev_t, dev_e),
            device_id_type=MESH,
        )

    ids = ids_ref[...]
    gates = gates_ref[...].astype(F32)
    row_e = iota((msg_rows, rows), 0) // group
    hits = jnp.zeros((msg_rows, rows), F32)
    weights = jnp.zeros((msg_rows, rows), F32)
    for k in range(ids.shape[0]):
        same = ids[k : k + 1, :] == row_e
        hits = hits + jnp.where(same, 1.0, 0.0)
        weights = weights + jnp.where(same, gates[k : k + 1, :], 0.0)
    earlier = jnp.where(iota((rows, rows), 0) < iota((rows, rows), 1), 1.0, 0.0)
    before = dot(hits.astype(BF16), earlier.astype(BF16))
    slot_of_row = lax.rem(iota((msg_rows, rows), 0), CAP).astype(F32)
    here = before == slot_of_row
    spread = jnp.where(
        iota((rows, PIECES * rows), 0) == lax.rem(iota((rows, PIECES * rows), 1), rows), 1.0, 0.0
    ).astype(BF16)
    wide = (msg_rows, PIECES * rows)
    same_piece = lax.rem(iota(wide, 0), group) // CAP == iota(wide, 1) // rows

    def table(values):
        full = dot(jnp.where(here, values, 0.0).astype(BF16), spread)
        return jnp.where(same_piece, full, 0.0).astype(BF16)

    pick_table = table(hits)
    for copy in loads[0]:
        copy.wait()
    slab[0] = (
        dot(pick_table, src[0]).astype(BF16).reshape(experts, group, width)
    )
    pl.semaphore_wait(barrier, experts + 2)

    def exchange(n):
        copies = []
        for k in range(1, experts):
            peer = lax.rem(e + k, experts)
            copies.append(
                remote(
                    slab.at[n, peer], land.at[n, e], a2a_send.at[n], a2a_recv.at[n], t, peer
                )
            )
        for copy in copies:
            copy.start()
        pltpu.make_async_copy(slab.at[n, e], land.at[n, e], own_sem.at[n]).start()

    def exchanged(n):
        pltpu.make_async_copy(slab.at[n, e], land.at[n, e], own_sem.at[n]).wait()
        some = pl.ds(0, experts - 1)
        whole = remote(
            slab.at[n, some], land.at[n, some], a2a_send.at[n], a2a_recv.at[n], t, e
        )
        whole.wait_send()
        whole.wait_recv()

    exchange(0)
    weight_table = table(weights)
    for copy in loads[1]:
        copy.wait()
    slab[1] = dot(weight_table, src[1]).astype(BF16).reshape(experts, group, width)
    exchange(1)

    square = (msg_rows, msg_rows)
    r0, r1 = iota(square, 0), iota(square, 1)
    gathers = jnp.where(
        r1 == lax.rem(r0, slots) // CAP * group + r0 // slots * CAP + lax.rem(r0, CAP), 1.0, 0.0
    ).astype(BF16)
    scatters = jnp.where(
        r1 == lax.rem(r0, group) // CAP * slots + r0 // group * CAP + lax.rem(r0, CAP), 1.0, 0.0
    ).astype(BF16)

    def take_rows(q):
        exchanged(q)
        own = dot(gathers, land[q].reshape(msg_rows, width)).astype(BF16)
        own = own.reshape(PIECES, 2, experts, width)
        for j in range(PIECES):
            x[q, t, :, :, j * width : (j + 1) * width] = own[j]

    def ag(q, n):
        block, half, dev = (
            (t, 0, up),
            (t, 1, up),
            (dn, 0, up),
            (t, 1, dn),
            (t, 0, dn),
            (up, 1, dn),
            (t, None, mate_t),
            (dn, 0, mate_t),
            (up, 1, mate_t),
            (dn, 1, mate_t),
            (up, 0, mate_t),
            (opp, 0, mate_t),
            (opp, 1, mate_t),
        )[n]
        ref = x.at[q, block] if half is None else x.at[q, block, half]
        return remote(ref, ref, ag_send.at[q, n], ag_recv.at[q, n], dev, e)

    def ag_arrived(q, n):
        mate_blocks = [lax.rem(mate_t + d, 8) for d in (0, 6, 2, 6, 2, 4, 4)]
        block, half = (
            (dn, 0),
            (dn, 1),
            (opp, 0),
            (up, 1),
            (up, 0),
            (opp, 1),
            (mate_blocks[0], None),
            (mate_blocks[1], 0),
            (mate_blocks[2], 1),
            (mate_blocks[3], 1),
            (mate_blocks[4], 0),
            (mate_blocks[5], 0),
            (mate_blocks[6], 1),
        )[n]
        ref = x.at[q, block] if half is None else x.at[q, block, half]
        remote(ref, ref, ag_send.at[q, n], ag_recv.at[q, n], t, e).wait_recv()

    def ag_first(q):
        for n in (0, 3, 1, 4, 6):
            ag(q, n).start()

    def ag_relay(q):
        ag_arrived(q, 0)
        ag(q, 2).start()
        ag(q, 7).start()
        ag_arrived(q, 3)
        ag(q, 5).start()
        ag(q, 8).start()

    def ag_second(q):
        ag_arrived(q, 1)
        ag(q, 9).start()
        ag_arrived(q, 4)
        ag(q, 10).start()

    def ag_last(q):
        ag_arrived(q, 2)
        ag(q, 11).start()
        ag_arrived(q, 5)
        ag(q, 12).start()
        for n in range(6, 13):
            ag_arrived(q, n)

    def rs(q, n):
        if n >= 6:
            d = (2, 1, 3, 0)[n - 6]
            a, b, dev = part.at[q, lax.rem(mate_t + 2 * d, 8)], mate.at[q, d], mate_t
        else:
            a, b, dev = (
                (summed.at[q, 2, 0], far.at[q, 0], up),
                (summed.at[q, 1, 1], near.at[q, 0, 1], up),
                (summed.at[q, 1, 0], near.at[q, 0, 0], up),
                (summed.at[q, 2, 1], far.at[q, 1], dn),
                (summed.at[q, 3, 0], near.at[q, 1, 0], dn),
                (summed.at[q, 3, 1], near.at[q, 1, 1], dn),
            )[n]
        return remote(a, b, rs_send.at[q, n], rs_recv.at[q, n], dev, e)

    def chip_sum(q, n):
        rs(q, n).wait_recv()
        d = (2, 1, 3, 0)[n - 6]
        own = part[q, lax.rem(t + 2 * d, 8)].astype(F32)
        summed[q, d] = (own + mate[q, d].astype(F32)).astype(BF16)

    def rs_pair(q):
        for n in range(6, 10):
            rs(q, n).start()

    def rs_first(q):
        chip_sum(q, 6)
        rs(q, 0).start()
        rs(q, 3).start()
        chip_sum(q, 7)
        rs(q, 1).start()
        chip_sum(q, 8)
        rs(q, 4).start()

    def rs_second(q):
        for way, d, half, n in ((0, 1, 0, 0), (1, 3, 1, 3)):
            rs(q, n).wait_recv()
            total = summed[q, d, half].astype(F32) + far[q, way].astype(F32)
            summed[q, d, half] = total.astype(BF16)
            rs(q, n + 2).start()

    def rs_last(q):
        rs(q, 9).wait_recv()
        for n in (1, 2, 4, 5):
            rs(q, n).wait_recv()
        total = part[q, t].astype(F32) + mate[q, 0].astype(F32)
        total = total + near[q, 0].astype(F32) + near[q, 1].astype(F32)
        total = total.astype(BF16)
        stacked = jnp.concatenate(
            [
                total[:, :, j * width : (j + 1) * width].reshape(slots, width)
                for j in range(PIECES)
            ],
            axis=0,
        )
        slab[2 + q] = dot(scatters, stacked).astype(BF16).reshape(experts, group, width)
        exchange(2 + q)

    def combine(q, placed):
        exchanged(2 + q)
        rows_out = dot_tn(placed, land[2 + q].reshape(msg_rows, width)).astype(BF16)
        for j in range(PIECES):
            outs[q, :, j * width : (j + 1) * width] = rows_out[j * rows : (j + 1) * rows]
        copy = pltpu.make_async_copy(
            outs.at[q], (moe_hbm, tgr_hbm)[q], out_sem.at[q]
        )
        copy.start()
        return copy

    def columns(k):
        return pl.ds(pl.multiple_of(k * width, width), width)

    def over_columns(step):
        def body(k, carry):
            step(columns(k))
            return carry

        lax.fori_loop(0, PIECES, body, 0)

    take_rows(0)
    ag_first(0)
    take_rows(1)
    ag_relay(0)
    ag_first(1)
    ag_second(0)
    load_win.wait()
    load_wdn.wait()
    ag_last(0)

    act[...] = jnp.zeros_like(act)

    def forward(cols):
        piece = x[0, :, :, :, cols].reshape(all_rows, width)
        act[0] += dot_nt(win[0, :, cols], piece)
        act[1] += dot_nt(win[1, :, cols], piece)

    over_columns(forward)
    ag_relay(1)
    gate = act[0]
    hid[0] = (gate * jax.nn.sigmoid(gate) * act[1]).astype(BF16)

    def terms_out(cols):
        piece = dot_tn(hid[0], wdn[:, cols]).astype(BF16)
        part[0, :, :, :, cols] = piece.reshape(8, 2, experts, width)

    over_columns(terms_out)
    rs_pair(0)
    ag_second(1)
    rs_first(0)
    ag_last(1)

    def backward(cols):
        piece = x[1, :, :, :, cols].reshape(all_rows, width)
        act[2] += dot_nt(wdn[:, cols], piece)

    over_columns(backward)
    gate = act[0]
    sigmoid = jax.nn.sigmoid(gate)
    grad = act[2]
    hid[1] = (grad * act[1] * sigmoid * (1.0 + gate * (1.0 - sigmoid))).astype(BF16)
    hid[2] = (grad * (gate * sigmoid)).astype(BF16)
    rs_second(0)

    def terms_grad(cols):
        piece = dot_tn(hid[1], win[0, :, cols]) + dot_tn(hid[2], win[1, :, cols])
        part[1, :, :, :, cols] = piece.astype(BF16).reshape(8, 2, experts, width)

    over_columns(terms_grad)
    rs_pair(1)
    rs_first(1)
    rs_last(0)

    def weights_down(cols):
        piece = x[1, :, :, :, cols].reshape(all_rows, width)
        gdn[:, cols] = dot(hid[0], piece).astype(BF16)

    def weights_in(cols):
        piece = x[0, :, :, :, cols].reshape(all_rows, width)
        gin[0, :, cols] = dot(hid[1], piece).astype(BF16)
        gin[1, :, cols] = dot(hid[2], piece).astype(BF16)

    over_columns(weights_down)
    store_gdn = pltpu.make_async_copy(gdn, gdn_hbm.at[0], out_sem.at[2])
    store_gdn.start()
    rs_second(1)
    over_columns(weights_in)
    store_gin = pltpu.make_async_copy(gin, gin_hbm.at[0], out_sem.at[3])
    store_gin.start()
    store_moe = combine(0, weight_table)
    rs_last(1)
    store_tgr = combine(1, pick_table)

    for q in range(2):
        for n in range(13):
            ag(q, n).wait_send()
        for n in range(10):
            rs(q, n).wait_send()
    for copy in (store_gdn, store_gin, store_moe, store_tgr):
        copy.wait()


def body(tokens, cotangent, expert_ids, gate_weights, w_in, w_down):
    experts = lax.axis_size("exp")
    rows, dim = tokens.shape
    ff = w_down.shape[1]
    width = dim // PIECES
    group = CAP * PIECES
    any_space = pl.BlockSpec(memory_space=pl.ANY)
    vmem = pl.BlockSpec(memory_space=pltpu.VMEM)
    shape = jax.ShapeDtypeStruct
    dma = pltpu.SemaphoreType.DMA
    return pl.pallas_call(
        functools.partial(kernel, experts),
        out_shape=(
            shape(tokens.shape, BF16),
            shape(tokens.shape, BF16),
            shape(w_in.shape, BF16),
            shape(w_down.shape, BF16),
        ),
        in_specs=[vmem, vmem, any_space, any_space, any_space, any_space],
        out_specs=(any_space,) * 4,
        scratch_shapes=[
            pltpu.VMEM((2, PIECES * rows, width), BF16),
            pltpu.VMEM((2, ff, dim), BF16),
            pltpu.VMEM((ff, dim), BF16),
            pltpu.VMEM((4, experts, group, width), BF16),
            pltpu.VMEM((4, experts, group, width), BF16),
            pltpu.VMEM((2, 8, 2, experts, dim), BF16),
            pltpu.VMEM((3, ff, 16 * experts), F32),
            pltpu.VMEM((3, ff, 16 * experts), BF16),
            pltpu.VMEM((2, 8, 2, experts, dim), BF16),
            pltpu.VMEM((2, 4, 2, experts, dim), BF16),
            pltpu.VMEM((2, 4, 2, experts, dim), BF16),
            pltpu.VMEM((2, 2, experts, dim), BF16),
            pltpu.VMEM((2, 2, 2, experts, dim), BF16),
            pltpu.VMEM((2, ff, dim), BF16),
            pltpu.VMEM((ff, dim), BF16),
            pltpu.VMEM((2, rows, dim), BF16),
            dma((2 * PIECES + 2,)),
            dma((4,)),
            dma((4,)),
            dma((4,)),
            dma((4,)),
            dma((2, 13)),
            dma((2, 13)),
            dma((2, 10)),
            dma((2, 10)),
        ],
        compiler_params=pltpu.CompilerParams(
            collective_id=0, has_side_effects=True, vmem_limit_bytes=60 * 1024 * 1024
        ),
    )(expert_ids.T, gate_weights.T, tokens, cotangent, w_in, w_down)


def solution(mesh):
    placed = (
        P(("tok", "exp"), None),
        P(("tok", "exp"), None),
        P(("tok", "exp"), None),
        P(("tok", "exp"), None),
        P("exp", None, "tok", None),
        P("exp", "tok", None),
    )
    return jax.shard_map(
        body,
        mesh=mesh,
        in_specs=placed,
        out_specs=(
            P(("tok", "exp"), None),
            P(("tok", "exp"), None),
            P("exp", None, "tok", None),
            P("exp", "tok", None),
        ),
        check_vma=False,
    )
```

```python
import functools

import jax
import jax.numpy as jnp
from jax import lax
from jax.experimental import pallas as pl
from jax.experimental.pallas import tpu as pltpu
from jax.sharding import PartitionSpec as P

CAP = 2
PIECES = 8
BF16 = jnp.bfloat16
F32 = jnp.float32
VMEM_LIMIT = 61_270_000
SPLITS = (4, 2, 2, 4)
MESH = pl.DeviceIdType.MESH


def dot(a, b):
    return jnp.dot(a, b, preferred_element_type=F32)


def dot_nt(a, b):
    return lax.dot_general(a, b, (((1,), (1,)), ((), ())), preferred_element_type=F32)


def dot_tn(a, b):
    return lax.dot_general(a, b, (((0,), (0,)), ((), ())), preferred_element_type=F32)


def iota(shape, dim):
    return lax.broadcasted_iota(jnp.int32, shape, dim)


def kernel(
    experts,
    ids_hbm,
    gates_hbm,
    tok_hbm,
    cot_hbm,
    win_hbm,
    wdn_hbm,
    moe,
    tgr,
    gin,
    gdn,
    ids_ref,
    gates_ref,
    src,
    win,
    wdn,
    x,
    act,
    hid,
    hid_rows,
    part,
    mate,
    summed,
    far,
    near,
    back,
    in_sem,
    a2a_send,
    a2a_recv,
    ag_send,
    ag_recv,
    rs_send,
    rs_recv,
    *boxes,
):
    slab, land = boxes[:4], boxes[4:]
    rows, dim = tok_hbm.shape
    group = CAP * PIECES
    slots = CAP * experts
    msg_rows = experts * group
    all_rows = 8 * slots
    chunk = dim // 8

    t = lax.axis_index("tok")
    e = lax.axis_index("exp")
    up = lax.rem(t + 2, 8)
    opp = lax.rem(t + 4, 8)
    dn = lax.rem(t + 6, 8)
    mate_t = t + 1 - 2 * lax.rem(t, 2)

    side = 4 if experts == 16 else 1
    line = experts // side

    def steps(k):
        a, b = k // line, k % line
        return min(a, side - a) + min(b, line - b)

    peers = [
        lax.rem(e // line + k // line, side) * line + lax.rem(lax.rem(e, line) + k % line, line)
        for k in sorted(range(1, experts), key=steps, reverse=True)
    ]
    barrier = pltpu.get_barrier_semaphore()
    for peer in peers:
        pl.semaphore_signal(barrier, inc=1, device_id=(t, peer), device_id_type=MESH)
    for other in (up, dn, mate_t):
        pl.semaphore_signal(barrier, inc=1, device_id=(other, e), device_id_type=MESH)

    loads = [
        pltpu.make_async_copy(a, b, in_sem.at[i])
        for i, (a, b) in enumerate(
            (
                (ids_hbm, ids_ref),
                (gates_hbm, gates_ref),
                (tok_hbm, src.at[0]),
                (cot_hbm, src.at[1]),
                (win_hbm.at[0], win),
                (wdn_hbm.at[0], wdn),
            )
        )
    ]
    for copy in loads:
        copy.start()

    def remote(a, b, ssem, rsem, dev_t, dev_e):
        return pltpu.make_async_remote_copy(
            src_ref=a,
            dst_ref=b,
            send_sem=ssem,
            recv_sem=rsem,
            device_id=(dev_t, dev_e),
            device_id_type=MESH,
        )

    loads[0].wait()
    loads[1].wait()
    ids = ids_ref[...]
    gates = gates_ref[...].astype(F32)
    row_e = iota((msg_rows, rows), 0) // group
    hits = jnp.zeros((msg_rows, rows), F32)
    weights = jnp.zeros((msg_rows, rows), F32)
    for k in range(ids.shape[0]):
        same = ids[k : k + 1, :] == row_e
        hits = hits + jnp.where(same, 1.0, 0.0)
        weights = weights + jnp.where(same, gates[k : k + 1, :], 0.0)
    earlier = jnp.where(iota((rows, rows), 0) < iota((rows, rows), 1), 1.0, 0.0)
    before = dot(hits.astype(BF16), earlier.astype(BF16))
    slot_of_row = lax.rem(iota((msg_rows, rows), 0), CAP).astype(F32)
    here = before == slot_of_row
    picked = jnp.where(here, hits, 0.0).astype(BF16)
    weighted = jnp.where(here, weights, 0.0).astype(BF16)
    wide = (msg_rows, PIECES * rows)
    tall = wide[::-1]

    def ones_where(test):
        return jnp.where(test, 1.0, 0.0).astype(BF16)

    def table(values):
        spread = ones_where(
            iota((rows, wide[1]), 0) == lax.rem(iota((rows, wide[1]), 1), rows)
        )
        same = lax.rem(iota(wide, 0), group) // CAP == iota(wide, 1) // rows
        return jnp.where(same, dot(values, spread), 0.0).astype(BF16)

    def back_table(values):
        spread = ones_where(
            lax.rem(iota((wide[1], rows), 0), rows) == iota((wide[1], rows), 1)
        )
        same = lax.rem(iota(tall, 1), group) // CAP == iota(tall, 0) // rows
        return jnp.where(same, dot_nt(spread, values), 0.0).astype(BF16)

    def span(n, s):
        size = dim // SPLITS[n]
        return pl.ds(s * size, size), size // PIECES

    def fill(n, s, placed):
        start, width = span(n, s)[0].start, span(n, s)[1]
        pieces = jnp.concatenate(
            [src[n, :, start + j * width : start + (j + 1) * width] for j in range(PIECES)],
            axis=0,
        )
        slab[n][s] = dot(placed, pieces).astype(BF16).reshape(experts, group, width)

    def exchange(n, s):
        copies = [
            remote(
                slab[n].at[s, peer],
                land[n].at[s, e],
                a2a_send.at[n],
                a2a_recv.at[n, s],
                t,
                peer,
            )
            for peer in peers
        ]
        for copy in copies:
            copy.start()
        land[n][s, e] = slab[n][s, e]

    def exchanged(n, s):
        ref = land[n].at[s, pl.ds(0, experts - 1)]
        remote(ref, ref, a2a_send.at[n], a2a_recv.at[n, s], t, e).wait_recv()
        return land[n][s].reshape(msg_rows, span(n, s)[1])

    pick_table = table(picked)
    loads[2].wait()
    for s in range(SPLITS[0]):
        fill(0, s, pick_table)
    pl.semaphore_wait(barrier, experts + 2)
    for s in range(SPLITS[0]):
        exchange(0, s)
    weight_table = table(weighted)
    loads[3].wait()
    for s in range(SPLITS[1]):
        fill(1, s, weight_table)
    for s in range(SPLITS[1]):
        exchange(1, s)

    square = (msg_rows, msg_rows)
    r0, r1 = iota(square, 0), iota(square, 1)
    gathers = ones_where(
        r1 == lax.rem(r0, slots) // CAP * group + r0 // slots * CAP + lax.rem(r0, CAP)
    )
    scatters = ones_where(
        r1 == lax.rem(r0, group) // CAP * slots + r0 // group * CAP + lax.rem(r0, CAP)
    )

    def take_rows(q, s):
        start, width = span(q, s)[0].start, span(q, s)[1]
        own = dot(gathers, exchanged(q, s)).astype(BF16)
        own = own.reshape(PIECES, 2, experts, width)
        for j in range(PIECES):
            x[q, t, :, :, start + j * width : start + (j + 1) * width] = own[j]

    def ag_ref(q, s, block, half):
        cols = span(q, s)[0]
        if half is None:
            return x.at[q, block, :, :, cols]
        return x.at[q, block, half, :, cols]

    def ag(q, s, n):
        block, half, dev = (
            (t, 0, up),
            (t, 1, up),
            (dn, 0, up),
            (t, 1, dn),
            (t, 0, dn),
            (up, 1, dn),
            (t, None, mate_t),
            (dn, 0, mate_t),
            (up, 1, mate_t),
            (dn, 1, mate_t),
            (up, 0, mate_t),
            (opp, 0, mate_t),
            (opp, 1, mate_t),
        )[n]
        ref = ag_ref(q, s, block, half)
        return remote(ref, ref, ag_send.at[q], ag_recv.at[q, s, n % 3 if n < 6 else 3], dev, e)

    def ag_arrived(q, s, n):
        ref = x.at[q, pl.ds(0, 4 if n == 3 else 1), :, :, span(q, s)[0]]
        remote(ref, ref, ag_send.at[q], ag_recv.at[q, s, n], t, e).wait_recv()

    def ag_first(q, s):
        for n in (0, 3, 1, 4, 6):
            ag(q, s, n).start()

    def ag_relay(q, s):
        ag_arrived(q, s, 0)
        for n in (2, 5, 7, 8):
            ag(q, s, n).start()

    def ag_second(q, s):
        ag_arrived(q, s, 1)
        for n in (9, 10):
            ag(q, s, n).start()

    def ag_third(q, s):
        ag_arrived(q, s, 2)
        for n in (11, 12):
            ag(q, s, n).start()

    def ag_last(q, s):
        ag_arrived(q, s, 3)

    def rs(q, s, n):
        cols = span(2 + q, s)[0]
        if n >= 6:
            d = (2, 1, 3, 0)[n - 6]
            a = part.at[q, lax.rem(mate_t + 2 * d, 8), :, :, cols]
            b, dev = mate.at[q, d, :, :, cols], mate_t
        else:
            a, b, dev = (
                (summed.at[q, 2, 0, :, cols], far.at[q, 0, :, cols], up),
                (summed.at[q, 1, 1, :, cols], near.at[q, 0, 1, :, cols], up),
                (summed.at[q, 1, 0, :, cols], near.at[q, 0, 0, :, cols], up),
                (summed.at[q, 2, 1, :, cols], far.at[q, 1, :, cols], dn),
                (summed.at[q, 3, 0, :, cols], near.at[q, 1, 0, :, cols], dn),
                (summed.at[q, 3, 1, :, cols], near.at[q, 1, 1, :, cols], dn),
            )[n]
        kind = (0, 1, 1, 0, 1, 1, 2, 3, 3, 3)[n]
        return remote(a, b, rs_send.at[q], rs_recv.at[q, s, kind], dev, e)

    def rs_arrived(q, s, kind):
        ref = (far.at[q], near.at[q], mate.at[q, 0], mate.at[q, pl.ds(0, 3)])[kind]
        ref = ref.at[..., span(2 + q, s)[0]]
        remote(ref, ref, rs_send.at[q], rs_recv.at[q, s, kind], t, e).wait_recv()

    def rs_pair(q, s):
        for n in range(6, 10):
            rs(q, s, n).start()

    def chip_sum(q, s, d):
        cols = span(2 + q, s)[0]
        own = part[q, lax.rem(t + 2 * d, 8), :, :, cols].astype(F32)
        summed[q, d, :, :, cols] = (own + mate[q, d, :, :, cols].astype(F32)).astype(BF16)

    def rs_far(q, s):
        rs_arrived(q, s, 2)
        chip_sum(q, s, 2)
        rs(q, s, 0).start()
        rs(q, s, 3).start()

    def rs_near(q, s):
        rs_arrived(q, s, 3)
        chip_sum(q, s, 1)
        rs(q, s, 1).start()
        chip_sum(q, s, 3)
        rs(q, s, 4).start()

    def rs_second(q, s):
        cols = span(2 + q, s)[0]
        rs_arrived(q, s, 0)
        for way, d, half, n in ((0, 1, 0, 2), (1, 3, 1, 5)):
            total = summed[q, d, half, :, cols].astype(F32) + far[q, way, :, cols].astype(F32)
            summed[q, d, half, :, cols] = total.astype(BF16)
            rs(q, s, n).start()

    def rs_last(q, s):
        cols, width = span(2 + q, s)
        total = part[q, t, :, :, cols].astype(F32) + mate[q, 0, :, :, cols].astype(F32)
        rs_arrived(q, s, 1)
        total = total + near[q, 0, :, :, cols].astype(F32) + near[q, 1, :, :, cols].astype(F32)
        total = total.astype(BF16).reshape(slots, PIECES * width)
        stacked = jnp.concatenate(
            [total[:, j * width : (j + 1) * width] for j in range(PIECES)], axis=0
        )
        slab[2 + q][s] = dot(scatters, stacked).astype(BF16).reshape(experts, group, width)
        exchange(2 + q, s)

    def combine(q, s):
        start, width = span(2 + q, s)[0].start, span(2 + q, s)[1]
        rows_out = dot(back[1 - q], exchanged(2 + q, s)).astype(BF16)
        out = (moe, tgr)[q]
        for j in range(PIECES):
            out[:, start + j * width : start + (j + 1) * width] = rows_out[
                j * rows : (j + 1) * rows
            ]

    def over(first, count, step):
        def body(k, carry):
            step(pl.ds(pl.multiple_of(k * chunk, chunk), chunk))
            return carry

        if count == 1:
            step(pl.ds(first * chunk, chunk))
        else:
            lax.fori_loop(first, first + count, body, 0)

    def chunks(n, s, step):
        count = 8 // SPLITS[n]
        over(s * count, count, step)

    def forward(cols):
        piece = x[0, :, :, :, cols].reshape(all_rows, chunk)
        act[0] += dot_nt(win[0, :, cols], piece)
        act[1] += dot_nt(win[1, :, cols], piece)

    def terms_out(cols):
        piece = dot(hid_rows[0], wdn[:, cols]).astype(BF16)
        part[0, :, :, :, cols] = piece.reshape(8, 2, experts, chunk)

    def backward(cols):
        piece = x[1, :, :, :, cols].reshape(all_rows, chunk)
        act[2] += dot_nt(wdn[:, cols], piece)

    def terms_grad(cols):
        piece = dot(hid_rows[1], win[0, :, cols]) + dot(hid_rows[2], win[1, :, cols])
        part[1, :, :, :, cols] = piece.astype(BF16).reshape(8, 2, experts, chunk)

    def weights_down(cols):
        piece = x[1, :, :, :, cols].reshape(all_rows, chunk)
        gdn[0, :, cols] = dot(hid[0], piece).astype(BF16)

    def weights_in(cols):
        piece = x[0, :, :, :, cols].reshape(all_rows, chunk)
        gin[0, 0, :, cols] = dot(hid[1], piece).astype(BF16)
        gin[0, 1, :, cols] = dot(hid[2], piece).astype(BF16)

    def keep(i, value):
        hid[i] = value.astype(BF16)
        hid_rows[i] = value.T.astype(BF16)

    act[...] = jnp.zeros_like(act)
    for s in range(SPLITS[0]):
        take_rows(0, s)
        ag_first(0, s)
    ag_relay(0, 0)
    for s in range(SPLITS[1]):
        take_rows(1, s)
    for s in range(1, SPLITS[0]):
        ag_relay(0, s)
    for s in range(SPLITS[1]):
        ag_first(1, s)
    back[0] = back_table(picked)
    back[1] = back_table(weighted)
    loads[4].wait()
    loads[5].wait()
    for s in range(SPLITS[0]):
        ag_second(0, s)
    for s in range(SPLITS[0]):
        ag_third(0, s)
    for s in range(SPLITS[0]):
        ag_last(0, s)
        chunks(0, s, forward)
    ag_relay(1, 0)

    gate = act[0]
    keep(0, gate * jax.nn.sigmoid(gate) * act[1])
    for s in range(SPLITS[2]):
        chunks(2, s, terms_out)
        rs_pair(0, s)
    for s in range(1, SPLITS[1]):
        ag_relay(1, s)
    for s in range(SPLITS[1]):
        ag_second(1, s)
    for s in range(SPLITS[2]):
        rs_far(0, s)
        rs_near(0, s)
    for s in range(SPLITS[1]):
        ag_third(1, s)
        ag_last(1, s)
        chunks(1, s, backward)

    gate = act[0]
    sigmoid = jax.nn.sigmoid(gate)
    grad = act[2]
    keep(1, grad * act[1] * sigmoid * (1.0 + gate * (1.0 - sigmoid)))
    keep(2, grad * (gate * sigmoid))
    for s in range(SPLITS[2]):
        rs_second(0, s)
    last = SPLITS[3]
    for s in range(last):
        chunks(3, s, terms_grad)
        rs_pair(1, s)

    rs_far(1, 0)
    rs_near(1, 0)
    rs_far(1, 1)
    rs_near(1, 1)
    for s in range(2, last):
        rs_far(1, s)
        rs_second(1, s - 2)
    for s in range(SPLITS[2]):
        rs_last(0, s)
    for s in range(2, last):
        rs_near(1, s)
        if s < last - 1:
            rs_second(1, s)
    rs_last(1, 0)
    rs_second(1, last - 1)
    over(0, 8, weights_down)
    for s in range(1, last):
        rs_last(1, s)
    over(0, 8, weights_in)
    for s in range(SPLITS[2]):
        combine(0, s)
    for s in range(last - 1):
        combine(1, s)

    for q in range(2):
        ref = x.at[q, pl.ds(0, 7)]
        remote(ref, ref, ag_send.at[q], ag_recv.at[q, 0, 0], t, e).wait_send()
        remote(ref, ref, rs_send.at[q], rs_recv.at[q, 0, 0], t, e).wait_send()
    for n in range(4):
        ref = slab[n].at[:, pl.ds(0, experts - 1)]
        remote(ref, ref, a2a_send.at[n], a2a_recv.at[n, 0], t, e).wait_send()
    combine(1, last - 1)


def store(*refs):
    count = len(refs) // 2
    sem = refs[-1]
    copies = [
        pltpu.make_async_copy(a, b, sem.at[i])
        for i, (a, b) in enumerate(zip(refs[:count], refs[count : 2 * count]))
    ]
    for copy in copies:
        copy.start()
    for copy in copies:
        copy.wait()


def body(tokens, cotangent, expert_ids, gate_weights, w_in, w_down):
    experts = lax.axis_size("exp")
    rows, dim = tokens.shape
    ff = w_down.shape[1]
    group = CAP * PIECES
    hbm = pl.BlockSpec(memory_space=pltpu.HBM)
    vmem = pl.BlockSpec(memory_space=pltpu.VMEM)
    shape = jax.ShapeDtypeStruct
    dma = pltpu.SemaphoreType.DMA
    shapes = (tokens.shape, tokens.shape, w_in.shape, w_down.shape)
    most = max(SPLITS)
    boxes = [
        pltpu.VMEM((n, experts, group, dim // n // PIECES), BF16) for n in SPLITS
    ]
    results = pl.pallas_call(
        functools.partial(kernel, experts),
        out_shape=tuple(pltpu.VMEM(s, BF16) for s in shapes),
        in_specs=[hbm] * 6,
        out_specs=(vmem,) * 4,
        scratch_shapes=[
            pltpu.VMEM(expert_ids.shape[::-1], jnp.int32),
            pltpu.VMEM(expert_ids.shape[::-1], BF16),
            pltpu.VMEM((2, rows, dim), BF16),
            pltpu.VMEM((2, ff, dim), BF16),
            pltpu.VMEM((ff, dim), BF16),
            pltpu.VMEM((2, 8, 2, experts, dim), BF16),
            pltpu.VMEM((3, ff, 16 * experts), F32),
            pltpu.VMEM((3, ff, 16 * experts), BF16),
            pltpu.VMEM((3, 16 * experts, ff), BF16),
            pltpu.VMEM((2, 8, 2, experts, dim), BF16),
            pltpu.VMEM((2, 4, 2, experts, dim), BF16),
            pltpu.VMEM((2, 4, 2, experts, dim), BF16),
            pltpu.VMEM((2, 2, experts, dim), BF16),
            pltpu.VMEM((2, 2, 2, experts, dim), BF16),
            pltpu.VMEM((2, PIECES * rows, experts * group), BF16),
            dma((6,)),
            dma((4,)),
            dma((4, most)),
            dma((2,)),
            dma((2, max(SPLITS[:2]), 4)),
            dma((2,)),
            dma((2, max(SPLITS[2:]), 4)),
        ]
        + boxes * 2,
        compiler_params=pltpu.CompilerParams(
            collective_id=0, has_side_effects=True, vmem_limit_bytes=VMEM_LIMIT
        ),
    )(expert_ids.T, gate_weights.T, tokens, cotangent, w_in, w_down)
    return pl.pallas_call(
        store,
        out_shape=tuple(shape(s, BF16) for s in shapes),
        in_specs=[vmem] * 4,
        out_specs=(hbm,) * 4,
        scratch_shapes=[dma((4,))],
        compiler_params=pltpu.CompilerParams(vmem_limit_bytes=1024 * 1024),
    )(*results)


def solution(mesh):
    placed = (
        P(("tok", "exp"), None),
        P(("tok", "exp"), None),
        P(("tok", "exp"), None),
        P(("tok", "exp"), None),
        P("exp", None, "tok", None),
        P("exp", "tok", None),
    )
    return jax.shard_map(
        body,
        mesh=mesh,
        in_specs=placed,
        out_specs=(
            P(("tok", "exp"), None),
            P(("tok", "exp"), None),
            P("exp", None, "tok", None),
            P("exp", "tok", None),
        ),
        check_vma=False,
    )
```

```python
import functools

import jax
import jax.numpy as jnp
from jax import lax
from jax.experimental import pallas as pl
from jax.experimental.pallas import tpu as pltpu
from jax.sharding import PartitionSpec as P

CAP = 2
PIECES = 8
BF16 = jnp.bfloat16
F32 = jnp.float32
VMEM_LIMIT = 61_270_000
AHEAD = 2
BEHIND = 2
SPLITS = (4, 4, 4, 4)
MESH = pl.DeviceIdType.MESH


def dot(a, b):
    return jnp.dot(a, b, preferred_element_type=F32)


def dot_nt(a, b):
    return lax.dot_general(a, b, (((1,), (1,)), ((), ())), preferred_element_type=F32)


def dot_tn(a, b):
    return lax.dot_general(a, b, (((0,), (0,)), ((), ())), preferred_element_type=F32)


def iota(shape, dim):
    return lax.broadcasted_iota(jnp.int32, shape, dim)


def stream(n, s):
    return sum(SPLITS[:n]) + s


def kernel(
    experts,
    ids_hbm,
    gates_hbm,
    tok_hbm,
    cot_hbm,
    win_hbm,
    wdn_hbm,
    moe,
    tgr,
    gin,
    gdn,
    ids_ref,
    gates_ref,
    src,
    win,
    wdn,
    x,
    act,
    hid,
    hid_rows,
    part,
    mate,
    summed,
    far,
    near,
    back,
    in_sem,
    a2a_send,
    a2a_recv,
    ag_send,
    ag_recv,
    rs_send,
    rs_recv,
    ring,
    ringland,
    ring_send,
    ring_recv,
    spread_send,
    spread_recv,
    mate_send,
    backslab,
    backland,
    backfar,
    backnear,
    back_send,
    back_recv,
    backring_send,
    backring_recv,
    backmate_send,
    *boxes,
):
    slab, land = boxes[:4], boxes[4:]
    rows, dim = tok_hbm.shape
    group = CAP * PIECES
    slots = CAP * experts
    msg_rows = experts * group
    all_rows = 8 * slots
    chunk = dim // 8

    t = lax.axis_index("tok")
    e = lax.axis_index("exp")
    up = lax.rem(t + 2, 8)
    opp = lax.rem(t + 4, 8)
    dn = lax.rem(t + 6, 8)
    mate_t = t + 1 - 2 * lax.rem(t, 2)
    y = t // 2

    side = 4 if experts == 16 else 1
    line = experts // side

    def steps(k):
        a, b = k // line, k % line
        return min(a, side - a) + min(b, line - b)

    peers = [
        lax.rem(e // line + k // line, side) * line + lax.rem(lax.rem(e, line) + k % line, line)
        for k in sorted(range(1, experts), key=steps, reverse=True)
    ]
    barrier = pltpu.get_barrier_semaphore()
    for peer in peers:
        pl.semaphore_signal(barrier, inc=1, device_id=(t, peer), device_id_type=MESH)
    for other in (up, dn, mate_t):
        pl.semaphore_signal(barrier, inc=1, device_id=(other, e), device_id_type=MESH)

    loads = [
        pltpu.make_async_copy(a, b, in_sem.at[i])
        for i, (a, b) in enumerate(
            (
                (ids_hbm, ids_ref),
                (gates_hbm, gates_ref),
                (tok_hbm, src.at[0]),
                (cot_hbm, src.at[1]),
                (win_hbm.at[0], win),
                (wdn_hbm.at[0], wdn),
            )
        )
    ]
    for copy in loads:
        copy.start()

    def remote(a, b, ssem, rsem, dev_t, dev_e):
        return pltpu.make_async_remote_copy(
            src_ref=a,
            dst_ref=b,
            send_sem=ssem,
            recv_sem=rsem,
            device_id=(dev_t, dev_e),
            device_id_type=MESH,
        )

    loads[0].wait()
    loads[1].wait()
    ids = ids_ref[...]
    gates = gates_ref[...].astype(F32)
    row_e = iota((msg_rows, rows), 0) // group
    hits = jnp.zeros((msg_rows, rows), F32)
    weights = jnp.zeros((msg_rows, rows), F32)
    for k in range(ids.shape[0]):
        same = ids[k : k + 1, :] == row_e
        hits = hits + jnp.where(same, 1.0, 0.0)
        weights = weights + jnp.where(same, gates[k : k + 1, :], 0.0)
    earlier = jnp.where(iota((rows, rows), 0) < iota((rows, rows), 1), 1.0, 0.0)
    before = dot(hits.astype(BF16), earlier.astype(BF16))
    slot_of_row = lax.rem(iota((msg_rows, rows), 0), CAP).astype(F32)
    here = before == slot_of_row
    picked = jnp.where(here, hits, 0.0).astype(BF16)
    weighted = jnp.where(here, weights, 0.0).astype(BF16)
    wide = (msg_rows, PIECES * rows)
    tall = wide[::-1]

    def ones_where(test):
        return jnp.where(test, 1.0, 0.0).astype(BF16)

    def table(values):
        spread = ones_where(
            iota((rows, wide[1]), 0) == lax.rem(iota((rows, wide[1]), 1), rows)
        )
        same = lax.rem(iota(wide, 0), group) // CAP == iota(wide, 1) // rows
        return jnp.where(same, dot(values, spread), 0.0).astype(BF16)

    def back_table(values):
        spread = ones_where(
            lax.rem(iota((wide[1], rows), 0), rows) == iota((wide[1], rows), 1)
        )
        same = lax.rem(iota(tall, 1), group) // CAP == iota(tall, 0) // rows
        return jnp.where(same, dot_nt(spread, values), 0.0).astype(BF16)

    def span(n, s):
        size = dim // SPLITS[n]
        return pl.ds(s * size, size), size // PIECES

    def fill(n, s, placed):
        start, width = span(n, s)[0].start, span(n, s)[1]
        pieces = jnp.concatenate(
            [src[n, :, start + j * width : start + (j + 1) * width] for j in range(PIECES)],
            axis=0,
        )
        message = dot(placed, pieces).astype(BF16).reshape(experts, group, width)
        if n == 0 and s < AHEAD:
            ring[s, y] = message
        else:
            slab[n][s] = message

    def exchange(n, s):
        copies = [
            remote(
                slab[n].at[s, peer],
                land[n].at[s, e],
                a2a_send.at[n],
                a2a_recv.at[stream(n, s)],
                t,
                peer,
            )
            for peer in peers
        ]
        for copy in copies:
            copy.start()
        land[n][s, e] = slab[n][s, e]

    def exchanged(n, s):
        ref = land[n].at[s, pl.ds(0, experts - 1)]
        remote(ref, ref, a2a_send.at[n], a2a_recv.at[stream(n, s)], t, e).wait_recv()
        return land[n][s].reshape(msg_rows, span(n, s)[1])

    def ring_copy(s, n):
        d, half, dev = (
            (0, 0, up),
            (0, 1, up),
            (3, 0, up),
            (0, 1, dn),
            (0, 0, dn),
            (1, 1, dn),
        )[n]
        count = experts // 2
        ref = ring.at[s, lax.rem(y + d, 4), pl.ds(half * count, count)]
        return remote(ref, ref, ring_send, ring_recv.at[s, n % 3], dev, e)

    def ring_arrived(s, kind):
        ref = ring.at[s, 0]
        remote(ref, ref, ring_send, ring_recv.at[s, kind], t, e).wait_recv()

    def ring_first():
        for pair in ((0, 3), (1, 4)):
            for s in range(AHEAD):
                for n in pair:
                    ring_copy(s, n).start()

    def spread(s, d):
        block = lax.rem(y + d, 4)
        copies = [
            remote(
                ring.at[s, block, peer],
                ringland.at[s, d, e],
                spread_send,
                spread_recv.at[s, d],
                t,
                peer,
            )
            for peer in peers
        ]
        for copy in copies:
            copy.start()
        ringland[s, d, e] = ring[s, block, e]

    def ring_relay(s):
        ring_arrived(s, 0)
        for n in (2, 5):
            ring_copy(s, n).start()

    def ring_near(s):
        ring_arrived(s, 1)
        spread(s, 1)
        spread(s, 3)

    def ring_last(s):
        ring_arrived(s, 2)
        spread(s, 2)

    def ring_take(s, d):
        ref = ringland.at[s, d, pl.ds(0, experts - 1)]
        remote(ref, ref, spread_send, spread_recv.at[s, d], t, e).wait_recv()
        block = lax.rem(t + 2 * d, 8)
        put_rows(0, s, block, ringland[s, d])
        ref = x.at[0, block, :, :, span(0, s)[0]]
        remote(ref, ref, mate_send, ag_recv.at[stream(0, s), 3], mate_t, e).start()

    pick_table = table(picked)
    loads[2].wait()
    for s in range(SPLITS[0]):
        fill(0, s, pick_table)
    pl.semaphore_wait(barrier, experts + 2)
    ring_first()
    for s in range(AHEAD, SPLITS[0]):
        exchange(0, s)
    weight_table = table(weighted)
    loads[3].wait()
    for s in range(SPLITS[1]):
        fill(1, s, weight_table)
    for s in range(SPLITS[1]):
        exchange(1, s)
    for s in range(AHEAD):
        spread(s, 0)

    square = (msg_rows, msg_rows)
    r0, r1 = iota(square, 0), iota(square, 1)
    gathers = ones_where(
        r1 == lax.rem(r0, slots) // CAP * group + r0 // slots * CAP + lax.rem(r0, CAP)
    )
    scatters = ones_where(
        r1 == lax.rem(r0, group) // CAP * slots + r0 // group * CAP + lax.rem(r0, CAP)
    )

    def put_rows(q, s, block, message):
        start, width = span(q, s)[0].start, span(q, s)[1]
        own = dot(gathers, message.reshape(msg_rows, width)).astype(BF16)
        own = own.reshape(PIECES, 2, experts, width)
        for j in range(PIECES):
            x[q, block, :, :, start + j * width : start + (j + 1) * width] = own[j]

    def take_rows(q, s):
        put_rows(q, s, t, exchanged(q, s))

    def ag_ref(q, s, block, half):
        cols = span(q, s)[0]
        if half is None:
            return x.at[q, block, :, :, cols]
        return x.at[q, block, half, :, cols]

    def ag(q, s, n):
        block, half, dev = (
            (t, 0, up),
            (t, 1, up),
            (dn, 0, up),
            (t, 1, dn),
            (t, 0, dn),
            (up, 1, dn),
            (t, None, mate_t),
            (dn, 0, mate_t),
            (up, 1, mate_t),
            (dn, 1, mate_t),
            (up, 0, mate_t),
            (opp, 0, mate_t),
            (opp, 1, mate_t),
        )[n]
        ref = ag_ref(q, s, block, half)
        return remote(ref, ref, ag_send.at[q], ag_recv.at[stream(q, s), n % 3 if n < 6 else 3], dev, e)

    def ag_arrived(q, s, n):
        ref = x.at[q, pl.ds(0, 4 if n == 3 else 1), :, :, span(q, s)[0]]
        remote(ref, ref, ag_send.at[q], ag_recv.at[stream(q, s), n], t, e).wait_recv()

    def ag_first(q, s):
        for n in (0, 3, 1, 4, 6):
            ag(q, s, n).start()

    def ag_relay(q, s):
        ag_arrived(q, s, 0)
        for n in (2, 5, 7, 8):
            ag(q, s, n).start()

    def ag_second(q, s):
        ag_arrived(q, s, 1)
        for n in (9, 10):
            ag(q, s, n).start()

    def ag_third(q, s):
        ag_arrived(q, s, 2)
        for n in (11, 12):
            ag(q, s, n).start()

    def ag_last(q, s):
        ag_arrived(q, s, 3)

    last = SPLITS[3]
    behind = last - BEHIND

    def rs(q, s, n):
        cols = span(2 + q, s)[0]
        if n >= 6:
            d = (2, 1, 3, 0)[n - 6]
            a = part.at[q, lax.rem(mate_t + 2 * d, 8), :, :, cols]
            b, dev = mate.at[q, d, :, :, cols], mate_t
        else:
            a, b, dev = (
                (summed.at[q, 2, 0, :, cols], far.at[q, 0, :, cols], up),
                (summed.at[q, 1, 1, :, cols], near.at[q, 0, 1, :, cols], up),
                (summed.at[q, 1, 0, :, cols], near.at[q, 0, 0, :, cols], up),
                (summed.at[q, 2, 1, :, cols], far.at[q, 1, :, cols], dn),
                (summed.at[q, 3, 0, :, cols], near.at[q, 1, 0, :, cols], dn),
                (summed.at[q, 3, 1, :, cols], near.at[q, 1, 1, :, cols], dn),
            )[n]
        kind = (0, 1, 1, 0, 1, 1, 2, 3, 3, 3)[n]
        sem = backmate_send if q == 1 and s >= behind else rs_send.at[q]
        return remote(a, b, sem, rs_recv.at[stream(2 + q, s) - stream(2, 0), kind], dev, e)

    def rs_arrived(q, s, kind):
        ref = (far.at[q], near.at[q], mate.at[q, 0], mate.at[q, pl.ds(0, 3)])[kind]
        ref = ref.at[..., span(2 + q, s)[0]]
        remote(ref, ref, rs_send.at[q], rs_recv.at[stream(2 + q, s) - stream(2, 0), kind], t, e).wait_recv()

    def rs_pair(q, s):
        for n in range(6, 10):
            rs(q, s, n).start()

    def chip_sum(q, s, d):
        cols = span(2 + q, s)[0]
        own = part[q, lax.rem(t + 2 * d, 8), :, :, cols].astype(F32)
        summed[q, d, :, :, cols] = (own + mate[q, d, :, :, cols].astype(F32)).astype(BF16)

    def rs_far(q, s):
        rs_arrived(q, s, 2)
        chip_sum(q, s, 2)
        rs(q, s, 0).start()
        rs(q, s, 3).start()

    def rs_near(q, s):
        rs_arrived(q, s, 3)
        chip_sum(q, s, 1)
        rs(q, s, 1).start()
        chip_sum(q, s, 3)
        rs(q, s, 4).start()

    def rs_second(q, s):
        cols = span(2 + q, s)[0]
        rs_arrived(q, s, 0)
        for way, d, half, n in ((0, 1, 0, 2), (1, 3, 1, 5)):
            total = summed[q, d, half, :, cols].astype(F32) + far[q, way, :, cols].astype(F32)
            summed[q, d, half, :, cols] = total.astype(BF16)
            rs(q, s, n).start()

    def as_message(total, width):
        total = total.astype(BF16).reshape(slots, PIECES * width)
        stacked = jnp.concatenate(
            [total[:, j * width : (j + 1) * width] for j in range(PIECES)], axis=0
        )
        return dot(scatters, stacked).astype(BF16).reshape(experts, group, width)

    def back_spread(d):
        for s in range(behind, last):
            cols, width = span(3, s)
            b = s - behind
            if d != 3 and d != 0:
                rs_arrived(1, s, 2 if d == 2 else 3)
            own = part[1, lax.rem(t + 2 * d, 8), :, :, cols].astype(F32)
            backslab[b, d] = as_message(own + mate[1, d, :, :, cols].astype(F32), width)
            copies = [
                remote(
                    backslab.at[b, d, peer],
                    backland.at[b, d, e],
                    back_send,
                    back_recv.at[b, d],
                    t,
                    peer,
                )
                for peer in peers
            ]
            for copy in copies:
                copy.start()
            backland[b, d, e] = backslab[b, d, e]

    def back_arrived(s, d):
        ref = backland.at[s - behind, d, pl.ds(0, experts - 1)]
        remote(ref, ref, back_send, back_recv.at[s - behind, d], t, e).wait_recv()

    low, high = pl.ds(0, experts // 2), pl.ds(experts // 2, experts // 2)

    def back_ring(s, d, half, ref, kind, dev):
        remote(
            backland.at[s - behind, d, half],
            ref,
            backring_send,
            backring_recv.at[s - behind, kind],
            dev,
            e,
        ).start()

    def back_ring_arrived(s, kind):
        ref = backnear.at[s - behind] if kind else backland.at[s - behind, 0]
        remote(ref, ref, backring_send, backring_recv.at[s - behind, kind], t, e).wait_recv()

    def back_far(s):
        b = s - behind
        back_arrived(s, 2)
        back_ring(s, 2, low, backfar.at[b, 0], 0, up)
        back_ring(s, 2, high, backfar.at[b, 1], 0, dn)

    def back_near(s):
        b = s - behind
        back_arrived(s, 1)
        back_ring(s, 1, high, backnear.at[b, 0, high], 1, up)
        back_arrived(s, 3)
        back_ring(s, 3, low, backnear.at[b, 1, low], 1, dn)

    def back_second(s):
        b = s - behind
        back_ring_arrived(s, 0)
        for way, d, half, dev in ((0, 1, low, up), (1, 3, high, dn)):
            total = backland[b, d, half].astype(F32) + backfar[b, way].astype(F32)
            backland[b, d, half] = total.astype(BF16)
            back_ring(s, d, half, backnear.at[b, way, half], 1, dev)

    def back_last(s):
        b = s - behind
        back_arrived(s, 0)
        own = backland[b, 0].astype(F32)
        back_ring_arrived(s, 1)
        total = own + backnear[b, 0].astype(F32) + backnear[b, 1].astype(F32)
        put_out(1, s, total.astype(BF16).reshape(msg_rows, span(3, s)[1]))

    def rs_last(q, s):
        cols, width = span(2 + q, s)
        total = part[q, t, :, :, cols].astype(F32) + mate[q, 0, :, :, cols].astype(F32)
        rs_arrived(q, s, 1)
        total = total + near[q, 0, :, :, cols].astype(F32) + near[q, 1, :, :, cols].astype(F32)
        slab[2 + q][s] = as_message(total, width)
        exchange(2 + q, s)

    def combine(q, s):
        put_out(q, s, exchanged(2 + q, s))

    def put_out(q, s, message):
        start, width = span(2 + q, s)[0].start, span(2 + q, s)[1]
        rows_out = dot(back[1 - q], message).astype(BF16)
        out = (moe, tgr)[q]
        for j in range(PIECES):
            out[:, start + j * width : start + (j + 1) * width] = rows_out[
                j * rows : (j + 1) * rows
            ]

    def over(first, count, step):
        def body(k, carry):
            step(pl.ds(pl.multiple_of(k * chunk, chunk), chunk))
            return carry

        if count == 1:
            step(pl.ds(first * chunk, chunk))
        else:
            lax.fori_loop(first, first + count, body, 0)

    def chunks(n, s, step):
        count = 8 // SPLITS[n]
        over(s * count, count, step)

    def forward(cols):
        piece = x[0, :, :, :, cols].reshape(all_rows, chunk)
        act[0] += dot_nt(win[0, :, cols], piece)
        act[1] += dot_nt(win[1, :, cols], piece)

    def terms_out(cols):
        piece = dot(hid_rows[0], wdn[:, cols]).astype(BF16)
        part[0, :, :, :, cols] = piece.reshape(8, 2, experts, chunk)

    def backward(cols):
        piece = x[1, :, :, :, cols].reshape(all_rows, chunk)
        act[2] += dot_nt(wdn[:, cols], piece)

    def terms_grad(cols):
        piece = dot(hid_rows[1], win[0, :, cols]) + dot(hid_rows[2], win[1, :, cols])
        part[1, :, :, :, cols] = piece.astype(BF16).reshape(8, 2, experts, chunk)

    def weights_down(cols):
        piece = x[1, :, :, :, cols].reshape(all_rows, chunk)
        gdn[0, :, cols] = dot(hid[0], piece).astype(BF16)

    def weights_in(cols):
        piece = x[0, :, :, :, cols].reshape(all_rows, chunk)
        gin[0, 0, :, cols] = dot(hid[1], piece).astype(BF16)
        gin[0, 1, :, cols] = dot(hid[2], piece).astype(BF16)

    def keep(i, value):
        hid[i] = value.astype(BF16)
        hid_rows[i] = value.T.astype(BF16)

    act[...] = jnp.zeros_like(act)
    for s in range(AHEAD):
        ring_relay(s)
    later = range(AHEAD, SPLITS[0])
    for s in later:
        take_rows(0, s)
        ag_first(0, s)
    for s in range(AHEAD):
        ring_near(s)
    for s in range(SPLITS[1]):
        take_rows(1, s)
    for s in later:
        ag_relay(0, s)
        if s == AHEAD:
            for a in range(AHEAD):
                ring_last(a)
    for s in range(SPLITS[1]):
        ag_first(1, s)
    for s in range(AHEAD):
        ring_take(s, 0)
    for s in later:
        ag_second(0, s)
    back[0] = back_table(picked)
    back[1] = back_table(weighted)
    for s in later:
        ag_third(0, s)
    for s in range(AHEAD):
        ring_take(s, 1)
        ring_take(s, 3)
    loads[4].wait()
    loads[5].wait()
    for s in later:
        ag_last(0, s)
        chunks(0, s, forward)
    ag_relay(1, 0)
    for s in range(AHEAD):
        ring_take(s, 2)
    ag_relay(1, 1)
    for s in range(AHEAD):
        ag_last(0, s)
        chunks(0, s, forward)
    ag_relay(1, 2)

    gate = act[0]
    keep(0, gate * jax.nn.sigmoid(gate) * act[1])
    for s in range(SPLITS[2]):
        chunks(2, s, terms_out)
        rs_pair(0, s)
        if s == 1:
            ag_relay(1, 3)
        if s >= 2:
            rs_far(0, s - 2)
    for s in range(SPLITS[1]):
        ag_second(1, s)
    rs_far(0, 2)
    rs_far(0, 3)
    rs_near(0, 0)
    rs_near(0, 1)
    ag_third(1, 0)
    ag_third(1, 1)
    rs_near(0, 2)
    rs_near(0, 3)
    for s in range(SPLITS[1]):
        if s < 2:
            ag_third(1, s + 2)
        ag_last(1, s)
        chunks(1, s, backward)

    gate = act[0]
    sigmoid = jax.nn.sigmoid(gate)
    grad = act[2]
    keep(1, grad * act[1] * sigmoid * (1.0 + gate * (1.0 - sigmoid)))
    keep(2, grad * (gate * sigmoid))
    for s in range(last):
        chunks(3, s, terms_grad)
        rs_pair(1, s)
        if s < 2:
            rs_second(0, s)
        if s >= 2 and s - 2 < behind:
            rs_far(1, s - 2)
    rs_second(0, 2)
    for s in range(2, behind):
        rs_far(1, s)
    for s in range(min(2, behind)):
        rs_near(1, s)
    back_spread(2)
    rs_second(0, 3)
    back_spread(1)
    back_spread(3)
    over(0, 4, weights_down)
    for s in range(min(2, behind)):
        rs_second(1, s)
    back_spread(0)
    for s in range(2, behind):
        rs_near(1, s)
    over(4, 4, weights_down)
    back_far(behind)
    over(0, 4, weights_in)
    for s in range(behind + 1, last):
        back_far(s)
    for s in range(SPLITS[2]):
        rs_last(0, s)
    for s in range(2, behind):
        rs_second(1, s)
    for s in range(behind, last):
        back_near(s)
    for s in range(behind):
        rs_last(1, s)
    back_second(behind)
    over(4, 4, weights_in)
    for s in range(behind + 1, last):
        back_second(s)
    for s in range(SPLITS[2]):
        combine(0, s)
    for s in range(behind, last - 1):
        back_last(s)
    for s in range(behind):
        combine(1, s)

    def sent(ref, sem):
        remote(ref, ref, sem, ring_recv.at[0, 0], t, e).wait_send()

    ahead = AHEAD * (dim // SPLITS[0])
    sent(x.at[0, pl.ds(0, 7), :, :, pl.ds(ahead, dim - ahead)], ag_send.at[0])
    sent(x.at[1, pl.ds(0, 7)], ag_send.at[1])
    sent(x.at[0, pl.ds(0, 4), :, :, pl.ds(0, ahead)], mate_send)
    sent(ring.at[:, pl.ds(0, 3)], ring_send)
    sent(ringland.at[:, :, pl.ds(0, experts - 1)], spread_send)
    wait_cols = behind * (dim // last)
    sent(part.at[0, pl.ds(0, 7)], rs_send.at[0])
    sent(part.at[1, pl.ds(0, 7), :, :, pl.ds(0, wait_cols)], rs_send.at[1])
    sent(part.at[1, pl.ds(0, 4), :, :, pl.ds(wait_cols, dim - wait_cols)], backmate_send)
    sent(backslab.at[:, :, pl.ds(0, experts - 1)], back_send)
    sent(backslab.at[:, pl.ds(0, 3)], backring_send)
    for n, (first, end) in enumerate(
        ((AHEAD, SPLITS[0]), (0, SPLITS[1]), (0, SPLITS[2]), (0, behind))
    ):
        ref = slab[n].at[first:end, pl.ds(0, experts - 1)]
        sent(ref, a2a_send.at[n])
    back_last(last - 1)


def store(*refs):
    copies = [
        pltpu.make_async_copy(a, b, refs[-1].at[i])
        for i, (a, b) in enumerate(zip(refs[:4], refs[4:8]))
    ]
    for copy in copies:
        copy.start()
    for copy in copies:
        copy.wait()


def body(tokens, cotangent, expert_ids, gate_weights, w_in, w_down):
    experts = lax.axis_size("exp")
    rows, dim = tokens.shape
    ff = w_down.shape[1]
    group = CAP * PIECES
    hbm = pl.BlockSpec(memory_space=pltpu.HBM)
    vmem = pl.BlockSpec(memory_space=pltpu.VMEM)
    shape = jax.ShapeDtypeStruct
    dma = pltpu.SemaphoreType.DMA
    shapes = (tokens.shape, tokens.shape, w_in.shape, w_down.shape)
    boxes = [
        pltpu.VMEM((n, experts, group, dim // n // PIECES), BF16) for n in SPLITS
    ]
    results = pl.pallas_call(
        functools.partial(kernel, experts),
        out_shape=tuple(pltpu.VMEM(s, BF16) for s in shapes),
        in_specs=[hbm] * 6,
        out_specs=(vmem,) * 4,
        scratch_shapes=[
            pltpu.VMEM(expert_ids.shape[::-1], jnp.int32),
            pltpu.VMEM(expert_ids.shape[::-1], BF16),
            pltpu.VMEM((2, rows, dim), BF16),
            pltpu.VMEM((2, ff, dim), BF16),
            pltpu.VMEM((ff, dim), BF16),
            pltpu.VMEM((2, 8, 2, experts, dim), BF16),
            pltpu.VMEM((3, ff, 16 * experts), F32),
            pltpu.VMEM((3, ff, 16 * experts), BF16),
            pltpu.VMEM((3, 16 * experts, ff), BF16),
            pltpu.VMEM((2, 8, 2, experts, dim), BF16),
            pltpu.VMEM((2, 4, 2, experts, dim), BF16),
            pltpu.VMEM((2, 4, 2, experts, dim), BF16),
            pltpu.VMEM((2, 2, experts, dim), BF16),
            pltpu.VMEM((2, 2, 2, experts, dim), BF16),
            pltpu.VMEM((2, PIECES * rows, experts * group), BF16),
            dma((6,)),
            dma((4,)),
            dma((sum(SPLITS),)),
            dma((2,)),
            dma((sum(SPLITS[:2]), 4)),
            dma((2,)),
            dma((sum(SPLITS[2:]), 4)),
            pltpu.VMEM((AHEAD, 4) + boxes[0].shape[1:], BF16),
            pltpu.VMEM((AHEAD, 4) + boxes[0].shape[1:], BF16),
            dma(()),
            dma((AHEAD, 3)),
            dma(()),
            dma((AHEAD, 4)),
            dma(()),
            pltpu.VMEM((BEHIND, 4) + boxes[3].shape[1:], BF16),
            pltpu.VMEM((BEHIND, 4) + boxes[3].shape[1:], BF16),
            pltpu.VMEM((BEHIND, 2, experts // 2) + boxes[3].shape[2:], BF16),
            pltpu.VMEM((BEHIND, 2) + boxes[3].shape[1:], BF16),
            dma(()),
            dma((BEHIND, 4)),
            dma(()),
            dma((BEHIND, 2)),
            dma(()),
        ]
        + boxes * 2,
        compiler_params=pltpu.CompilerParams(
            collective_id=0, has_side_effects=True, vmem_limit_bytes=VMEM_LIMIT
        ),
    )(expert_ids.T, gate_weights.T, tokens, cotangent, w_in, w_down)
    return pl.pallas_call(
        store,
        out_shape=tuple(shape(s, BF16) for s in shapes),
        in_specs=[vmem] * 4,
        out_specs=(hbm,) * 4,
        scratch_shapes=[dma((4,))],
        compiler_params=pltpu.CompilerParams(vmem_limit_bytes=1024 * 1024),
    )(*results)


def solution(mesh):
    placed = (
        P(("tok", "exp"), None),
        P(("tok", "exp"), None),
        P(("tok", "exp"), None),
        P(("tok", "exp"), None),
        P("exp", None, "tok", None),
        P("exp", "tok", None),
    )
    return jax.shard_map(
        body,
        mesh=mesh,
        in_specs=placed,
        out_specs=(
            P(("tok", "exp"), None),
            P(("tok", "exp"), None),
            P("exp", None, "tok", None),
            P("exp", "tok", None),
        ),
        check_vma=False,
    )
```

```python
import functools

import jax
import jax.numpy as jnp
from jax import lax
from jax.experimental import pallas as pl
from jax.experimental.pallas import tpu as pltpu
from jax.sharding import PartitionSpec as P

CAP = 2
PIECES = 8
BF16 = jnp.bfloat16
F32 = jnp.float32
VMEM_LIMIT = 61_270_000
AHEAD = 2
CHUNKS = 4
BEHIND = 2
SPLITS = (4, 4, 4, 4)
MESH = pl.DeviceIdType.MESH


def dot(a, b):
    return jnp.dot(a, b, preferred_element_type=F32)


def dot_nt(a, b):
    return lax.dot_general(a, b, (((1,), (1,)), ((), ())), preferred_element_type=F32)


def dot_tn(a, b):
    return lax.dot_general(a, b, (((0,), (0,)), ((), ())), preferred_element_type=F32)


def iota(shape, dim):
    return lax.broadcasted_iota(jnp.int32, shape, dim)


def numbered(keys):
    return {key: i for i, key in enumerate(keys)}


A2A = numbered(
    (n, s)
    for n in range(4)
    for s in range(AHEAD if n == 0 else 0, SPLITS[n] - (BEHIND if n == 3 else 0))
)
GATHER = numbered(
    (q, s, kind)
    for q in range(2)
    for s in range(SPLITS[q])
    for kind in range(3 if q == 0 and s < AHEAD else 0, 4)
)
REDUCE = numbered(
    (q, s, kind)
    for q in range(2)
    for s in range(SPLITS[2 + q])
    for kind in range(2 if q == 1 and s >= SPLITS[3] - BEHIND else 0, 4)
)


def kernel(
    experts,
    ids_hbm,
    gates_hbm,
    tok_hbm,
    cot_hbm,
    win_hbm,
    wdn_hbm,
    moe,
    tgr,
    gin,
    gdn,
    ids_ref,
    gates_ref,
    src,
    win,
    wdn,
    x,
    act,
    hid,
    hid_rows,
    pair_rows,
    part,
    mate,
    summed,
    far,
    near,
    back,
    in_sem,
    a2a_send,
    a2a_recv,
    ag_send,
    ag_recv,
    rs_send,
    rs_recv,
    ring,
    ringland,
    ring_send,
    ring_recv,
    spread_send,
    spread_recv,
    mate_send,
    backslab,
    backland,
    backfar,
    backnear,
    back_send,
    back_recv,
    backring_send,
    backring_recv,
    backmate_send,
    *boxes,
):
    slab, land = boxes[:4], boxes[4:]
    rows, dim = tok_hbm.shape
    group = CAP * PIECES
    slots = CAP * experts
    msg_rows = experts * group
    all_rows = 8 * slots
    chunk = dim // CHUNKS
    ff = win.shape[1]

    t = lax.axis_index("tok")
    e = lax.axis_index("exp")
    up = lax.rem(t + 2, 8)
    opp = lax.rem(t + 4, 8)
    dn = lax.rem(t + 6, 8)
    mate_t = t + 1 - 2 * lax.rem(t, 2)
    y = t // 2

    side = 4 if experts == 16 else 1
    line = experts // side

    def steps(k):
        a, b = k // line, k % line
        return min(a, side - a) + min(b, line - b)

    peers = [
        lax.rem(e // line + k // line, side) * line + lax.rem(lax.rem(e, line) + k % line, line)
        for k in sorted(range(1, experts), key=steps, reverse=True)
    ]
    barrier = pltpu.get_barrier_semaphore()
    for peer in peers:
        pl.semaphore_signal(barrier, inc=1, device_id=(t, peer), device_id_type=MESH)
    for other in (up, dn, mate_t):
        pl.semaphore_signal(barrier, inc=1, device_id=(other, e), device_id_type=MESH)

    loads = [
        pltpu.make_async_copy(a, b, in_sem.at[i])
        for i, (a, b) in enumerate(
            (
                (ids_hbm, ids_ref),
                (gates_hbm, gates_ref),
                (tok_hbm, src.at[0]),
                (cot_hbm, src.at[1]),
                (win_hbm.at[0], win),
                (wdn_hbm.at[0], wdn),
            )
        )
    ]
    for copy in loads:
        copy.start()

    def remote(a, b, ssem, rsem, dev_t, dev_e):
        return pltpu.make_async_remote_copy(
            src_ref=a,
            dst_ref=b,
            send_sem=ssem,
            recv_sem=rsem,
            device_id=(dev_t, dev_e),
            device_id_type=MESH,
        )

    loads[0].wait()
    loads[1].wait()
    ids = ids_ref[...]
    gates = gates_ref[...].astype(F32)
    row_e = iota((msg_rows, rows), 0) // group
    hits = jnp.zeros((msg_rows, rows), F32)
    weights = jnp.zeros((msg_rows, rows), F32)
    for k in range(ids.shape[0]):
        same = ids[k : k + 1, :] == row_e
        hits = hits + jnp.where(same, 1.0, 0.0)
        weights = weights + jnp.where(same, gates[k : k + 1, :], 0.0)
    earlier = jnp.where(iota((rows, rows), 0) < iota((rows, rows), 1), 1.0, 0.0)
    before = dot(hits.astype(BF16), earlier.astype(BF16))
    slot_of_row = lax.rem(iota((msg_rows, rows), 0), CAP).astype(F32)
    here = before == slot_of_row
    picked = jnp.where(here, hits, 0.0).astype(BF16)
    weighted = jnp.where(here, weights, 0.0).astype(BF16)
    wide = (msg_rows, PIECES * rows)
    tall = wide[::-1]

    def ones_where(test):
        return jnp.where(test, 1.0, 0.0).astype(BF16)

    def table(values):
        spread = ones_where(
            iota((rows, wide[1]), 0) == lax.rem(iota((rows, wide[1]), 1), rows)
        )
        same = lax.rem(iota(wide, 0), group) // CAP == iota(wide, 1) // rows
        return jnp.where(same, dot(values, spread), 0.0).astype(BF16)

    def back_table(values):
        spread = ones_where(
            lax.rem(iota((wide[1], rows), 0), rows) == iota((wide[1], rows), 1)
        )
        same = lax.rem(iota(tall, 1), group) // CAP == iota(tall, 0) // rows
        return jnp.where(same, dot_nt(spread, values), 0.0).astype(BF16)

    def span(n, s):
        size = dim // SPLITS[n]
        return pl.ds(s * size, size), size // PIECES

    def fill(n, s, placed):
        start, width = span(n, s)[0].start, span(n, s)[1]
        pieces = jnp.concatenate(
            [src[n, :, start + j * width : start + (j + 1) * width] for j in range(PIECES)],
            axis=0,
        )
        message = dot(placed, pieces).astype(BF16).reshape(experts, group, width)
        if n == 0 and s < AHEAD:
            ring[s, y] = message
        else:
            slab[n][s] = message

    def exchange(n, s):
        copies = [
            remote(
                slab[n].at[s, peer],
                land[n].at[s, e],
                a2a_send.at[n],
                a2a_recv.at[A2A[n, s]],
                t,
                peer,
            )
            for peer in peers
        ]
        for copy in copies:
            copy.start()
        land[n][s, e] = slab[n][s, e]

    def exchanged(n, s):
        ref = land[n].at[s, pl.ds(0, experts - 1)]
        remote(ref, ref, a2a_send.at[n], a2a_recv.at[A2A[n, s]], t, e).wait_recv()
        return land[n][s].reshape(msg_rows, span(n, s)[1])

    def ring_copy(s, n):
        d, half, dev = (
            (0, 0, up),
            (0, 1, up),
            (3, 0, up),
            (0, 1, dn),
            (0, 0, dn),
            (1, 1, dn),
        )[n]
        count = experts // 2
        ref = ring.at[s, lax.rem(y + d, 4), pl.ds(half * count, count)]
        return remote(ref, ref, ring_send, ring_recv.at[s, n % 3], dev, e)

    def ring_arrived(s, kind):
        ref = ring.at[s, 0]
        remote(ref, ref, ring_send, ring_recv.at[s, kind], t, e).wait_recv()

    def ring_first():
        for pair in ((0, 3), (1, 4)):
            for s in range(AHEAD):
                for n in pair:
                    ring_copy(s, n).start()

    def spread(s, d):
        block = lax.rem(y + d, 4)
        copies = [
            remote(
                ring.at[s, block, peer],
                ringland.at[s, d, e],
                spread_send,
                spread_recv.at[s, d],
                t,
                peer,
            )
            for peer in peers
        ]
        for copy in copies:
            copy.start()
        ringland[s, d, e] = ring[s, block, e]

    def ring_relay(s):
        ring_arrived(s, 0)
        for n in (2, 5):
            ring_copy(s, n).start()

    def ring_near(s):
        ring_arrived(s, 1)
        spread(s, 1)
        spread(s, 3)

    def ring_last(s):
        ring_arrived(s, 2)
        spread(s, 2)

    def ring_take(s, d):
        ref = ringland.at[s, d, pl.ds(0, experts - 1)]
        remote(ref, ref, spread_send, spread_recv.at[s, d], t, e).wait_recv()
        block = lax.rem(t + 2 * d, 8)
        put_rows(0, s, block, ringland[s, d])
        ref = x.at[0, block, :, :, span(0, s)[0]]
        remote(ref, ref, mate_send, ag_recv.at[GATHER[0, s, 3]], mate_t, e).start()

    pick_table = table(picked)
    loads[2].wait()
    for s in range(SPLITS[0]):
        fill(0, s, pick_table)
    pl.semaphore_wait(barrier, experts + 2)
    ring_first()
    for s in range(AHEAD, SPLITS[0]):
        exchange(0, s)
    weight_table = table(weighted)
    loads[3].wait()
    for s in range(SPLITS[1]):
        fill(1, s, weight_table)
    for s in range(SPLITS[1]):
        exchange(1, s)
    for s in range(AHEAD):
        spread(s, 0)

    square = (msg_rows, msg_rows)
    r0, r1 = iota(square, 0), iota(square, 1)
    gathers = ones_where(
        r1 == lax.rem(r0, slots) // CAP * group + r0 // slots * CAP + lax.rem(r0, CAP)
    )
    scatters = ones_where(
        r1 == lax.rem(r0, group) // CAP * slots + r0 // group * CAP + lax.rem(r0, CAP)
    )

    def put_rows(q, s, block, message):
        start, width = span(q, s)[0].start, span(q, s)[1]
        own = dot(gathers, message.reshape(msg_rows, width)).astype(BF16)
        own = own.reshape(PIECES, 2, experts, width)
        for j in range(PIECES):
            x[q, block, :, :, start + j * width : start + (j + 1) * width] = own[j]

    def take_rows(q, s):
        put_rows(q, s, t, exchanged(q, s))

    def ag_ref(q, s, block, half):
        cols = span(q, s)[0]
        if half is None:
            return x.at[q, block, :, :, cols]
        return x.at[q, block, half, :, cols]

    def ag(q, s, n):
        block, half, dev = (
            (t, 0, up),
            (t, 1, up),
            (dn, 0, up),
            (t, 1, dn),
            (t, 0, dn),
            (up, 1, dn),
            (t, None, mate_t),
            (dn, 0, mate_t),
            (up, 1, mate_t),
            (dn, 1, mate_t),
            (up, 0, mate_t),
            (opp, 0, mate_t),
            (opp, 1, mate_t),
        )[n]
        ref = ag_ref(q, s, block, half)
        return remote(ref, ref, ag_send.at[q], ag_recv.at[GATHER[q, s, n % 3 if n < 6 else 3]], dev, e)

    def ag_arrived(q, s, n):
        ref = x.at[q, pl.ds(0, 4 if n == 3 else 1), :, :, span(q, s)[0]]
        remote(ref, ref, ag_send.at[q], ag_recv.at[GATHER[q, s, n]], t, e).wait_recv()

    def ag_first(q, s):
        for n in (0, 3, 1, 4, 6):
            ag(q, s, n).start()

    def ag_relay(q, s):
        ag_arrived(q, s, 0)
        for n in (2, 5, 7, 8):
            ag(q, s, n).start()

    def ag_second(q, s):
        ag_arrived(q, s, 1)
        for n in (9, 10):
            ag(q, s, n).start()

    def ag_third(q, s):
        ag_arrived(q, s, 2)
        for n in (11, 12):
            ag(q, s, n).start()

    def ag_last(q, s):
        ag_arrived(q, s, 3)

    last = SPLITS[3]
    behind = last - BEHIND

    def rs(q, s, n):
        cols = span(2 + q, s)[0]
        if n >= 6:
            d = (2, 1, 3, 0)[n - 6]
            a = part.at[q, lax.rem(mate_t + 2 * d, 8), :, :, cols]
            b, dev = mate.at[q, d, :, :, cols], mate_t
        else:
            a, b, dev = (
                (summed.at[q, 2, 0, :, cols], far.at[q, 0, :, cols], up),
                (summed.at[q, 1, 1, :, cols], near.at[q, 0, 1, :, cols], up),
                (summed.at[q, 1, 0, :, cols], near.at[q, 0, 0, :, cols], up),
                (summed.at[q, 2, 1, :, cols], far.at[q, 1, :, cols], dn),
                (summed.at[q, 3, 0, :, cols], near.at[q, 1, 0, :, cols], dn),
                (summed.at[q, 3, 1, :, cols], near.at[q, 1, 1, :, cols], dn),
            )[n]
        kind = (0, 1, 1, 0, 1, 1, 2, 3, 3, 3)[n]
        sem = backmate_send if q == 1 and s >= behind else rs_send.at[q]
        return remote(a, b, sem, rs_recv.at[REDUCE[q, s, kind]], dev, e)

    def rs_arrived(q, s, kind):
        ref = (far.at[q], near.at[q], mate.at[q, 0], mate.at[q, pl.ds(0, 3)])[kind]
        ref = ref.at[..., span(2 + q, s)[0]]
        remote(ref, ref, rs_send.at[q], rs_recv.at[REDUCE[q, s, kind]], t, e).wait_recv()

    def rs_pair(q, s):
        for n in range(6, 10):
            rs(q, s, n).start()

    def chip_sum(q, s, d):
        cols = span(2 + q, s)[0]
        own = part[q, lax.rem(t + 2 * d, 8), :, :, cols].astype(F32)
        summed[q, d, :, :, cols] = (own + mate[q, d, :, :, cols].astype(F32)).astype(BF16)

    def rs_far(q, s):
        rs_arrived(q, s, 2)
        chip_sum(q, s, 2)
        rs(q, s, 0).start()
        rs(q, s, 3).start()

    def rs_near(q, s):
        rs_arrived(q, s, 3)
        chip_sum(q, s, 1)
        rs(q, s, 1).start()
        chip_sum(q, s, 3)
        rs(q, s, 4).start()

    def rs_second(q, s):
        cols = span(2 + q, s)[0]
        rs_arrived(q, s, 0)
        for way, d, half, n in ((0, 1, 0, 2), (1, 3, 1, 5)):
            total = summed[q, d, half, :, cols].astype(F32) + far[q, way, :, cols].astype(F32)
            summed[q, d, half, :, cols] = total.astype(BF16)
            rs(q, s, n).start()

    def as_message(total, width):
        total = total.astype(BF16).reshape(slots, PIECES * width)
        stacked = jnp.concatenate(
            [total[:, j * width : (j + 1) * width] for j in range(PIECES)], axis=0
        )
        return dot(scatters, stacked).astype(BF16).reshape(experts, group, width)

    def back_spread(d):
        for s in range(behind, last):
            cols, width = span(3, s)
            b = s - behind
            if d != 3 and d != 0:
                rs_arrived(1, s, 2 if d == 2 else 3)
            own = part[1, lax.rem(t + 2 * d, 8), :, :, cols].astype(F32)
            backslab[b, d] = as_message(own + mate[1, d, :, :, cols].astype(F32), width)
            copies = [
                remote(
                    backslab.at[b, d, peer],
                    backland.at[b, d, e],
                    back_send,
                    back_recv.at[b, d],
                    t,
                    peer,
                )
                for peer in peers
            ]
            for copy in copies:
                copy.start()
            backland[b, d, e] = backslab[b, d, e]

    def back_arrived(s, d):
        ref = backland.at[s - behind, d, pl.ds(0, experts - 1)]
        remote(ref, ref, back_send, back_recv.at[s - behind, d], t, e).wait_recv()

    low, high = pl.ds(0, experts // 2), pl.ds(experts // 2, experts // 2)

    def back_ring(s, d, half, ref, kind, dev):
        remote(
            backland.at[s - behind, d, half],
            ref,
            backring_send,
            backring_recv.at[s - behind, kind],
            dev,
            e,
        ).start()

    def back_ring_arrived(s, kind):
        ref = backnear.at[s - behind] if kind else backland.at[s - behind, 0]
        remote(ref, ref, backring_send, backring_recv.at[s - behind, kind], t, e).wait_recv()

    def back_far(s):
        b = s - behind
        back_arrived(s, 2)
        back_ring(s, 2, low, backfar.at[b, 0], 0, up)
        back_ring(s, 2, high, backfar.at[b, 1], 0, dn)

    def back_near(s):
        b = s - behind
        back_arrived(s, 1)
        back_ring(s, 1, high, backnear.at[b, 0, high], 1, up)
        back_arrived(s, 3)
        back_ring(s, 3, low, backnear.at[b, 1, low], 1, dn)

    def back_second(s):
        b = s - behind
        back_ring_arrived(s, 0)
        for way, d, half, dev in ((0, 1, low, up), (1, 3, high, dn)):
            total = backland[b, d, half].astype(F32) + backfar[b, way].astype(F32)
            backland[b, d, half] = total.astype(BF16)
            back_ring(s, d, half, backnear.at[b, way, half], 1, dev)

    def back_last(s):
        b = s - behind
        back_arrived(s, 0)
        own = backland[b, 0].astype(F32)
        back_ring_arrived(s, 1)
        total = own + backnear[b, 0].astype(F32) + backnear[b, 1].astype(F32)
        put_out(1, s, total.astype(BF16).reshape(msg_rows, span(3, s)[1]))

    def rs_last(q, s):
        cols, width = span(2 + q, s)
        total = part[q, t, :, :, cols].astype(F32) + mate[q, 0, :, :, cols].astype(F32)
        rs_arrived(q, s, 1)
        total = total + near[q, 0, :, :, cols].astype(F32) + near[q, 1, :, :, cols].astype(F32)
        slab[2 + q][s] = as_message(total, width)
        exchange(2 + q, s)

    def combine(q, s):
        put_out(q, s, exchanged(2 + q, s))

    def put_out(q, s, message):
        start, width = span(2 + q, s)[0].start, span(2 + q, s)[1]
        rows_out = dot(back[1 - q], message).astype(BF16)
        out = (moe, tgr)[q]
        for j in range(PIECES):
            out[:, start + j * width : start + (j + 1) * width] = rows_out[
                j * rows : (j + 1) * rows
            ]

    def over(first, count, step):
        def body(k, carry):
            step(pl.ds(pl.multiple_of(k * chunk, chunk), chunk))
            return carry

        if count == 1:
            step(pl.ds(first * chunk, chunk))
        else:
            lax.fori_loop(first, first + count, body, 0)

    def chunks(n, s, step):
        count = CHUNKS // SPLITS[n]
        over(s * count, count, step)

    def forward(cols):
        piece = x[0, :, :, :, cols].reshape(all_rows, chunk)
        both = dot_nt(win[:, :, cols].reshape(2 * ff, chunk), piece)
        act[0:2] += both.reshape(2, ff, all_rows)

    def terms_out(cols):
        piece = dot(hid_rows[...], wdn[:, cols]).astype(BF16)
        part[0, :, :, :, cols] = piece.reshape(8, 2, experts, chunk)

    def backward(cols):
        piece = x[1, :, :, :, cols].reshape(all_rows, chunk)
        act[2] += dot_nt(wdn[:, cols], piece)

    def terms_grad(cols):
        piece = dot(pair_rows[...], win[:, :, cols].reshape(2 * ff, chunk))
        part[1, :, :, :, cols] = piece.astype(BF16).reshape(8, 2, experts, chunk)

    def weights_down(cols):
        piece = x[1, :, :, :, cols].reshape(all_rows, chunk)
        gdn[0, :, cols] = dot(hid[0], piece).astype(BF16)

    def weights_in(cols):
        piece = x[0, :, :, :, cols].reshape(all_rows, chunk)
        both = dot(hid[1:3].reshape(2 * ff, all_rows), piece).astype(BF16)
        gin[0, :, :, cols] = both.reshape(2, ff, chunk)

    def keep(i, value):
        hid[i] = value.astype(BF16)
        if i == 0:
            hid_rows[...] = value.T.astype(BF16)
        else:
            pair_rows[:, (i - 1) * ff : i * ff] = value.T.astype(BF16)

    act[...] = jnp.zeros_like(act)
    for s in range(AHEAD):
        ring_relay(s)
    later = range(AHEAD, SPLITS[0])
    for s in later:
        take_rows(0, s)
        ag_first(0, s)
    for s in range(AHEAD):
        ring_near(s)
    for s in range(SPLITS[1]):
        take_rows(1, s)
    for s in later:
        ag_relay(0, s)
        if s == AHEAD:
            for a in range(AHEAD):
                ring_last(a)
    for s in range(SPLITS[1]):
        ag_first(1, s)
    for s in range(AHEAD):
        ring_take(s, 0)
    for s in later:
        ag_second(0, s)
    back[0] = back_table(picked)
    back[1] = back_table(weighted)
    for s in later:
        ag_third(0, s)
    for s in range(AHEAD):
        ring_take(s, 1)
        ring_take(s, 3)
    loads[4].wait()
    loads[5].wait()
    for s in later:
        ag_last(0, s)
        chunks(0, s, forward)
    ag_relay(1, 0)
    for s in range(AHEAD):
        ring_take(s, 2)
    ag_relay(1, 1)
    for s in range(AHEAD):
        ag_last(0, s)
        chunks(0, s, forward)
    ag_relay(1, 2)

    gate = act[0]
    keep(0, gate * jax.nn.sigmoid(gate) * act[1])
    for s in range(SPLITS[2]):
        chunks(2, s, terms_out)
        rs_pair(0, s)
        if s == 1:
            ag_relay(1, 3)
        if s >= 2:
            rs_far(0, s - 2)
    for s in range(SPLITS[1]):
        ag_second(1, s)
    rs_far(0, 2)
    rs_far(0, 3)
    rs_near(0, 0)
    rs_near(0, 1)
    ag_third(1, 0)
    ag_third(1, 1)
    rs_near(0, 2)
    rs_near(0, 3)
    for s in range(SPLITS[1]):
        if s < 2:
            ag_third(1, s + 2)
        ag_last(1, s)
        chunks(1, s, backward)

    gate = act[0]
    sigmoid = jax.nn.sigmoid(gate)
    grad = act[2]
    keep(1, grad * act[1] * sigmoid * (1.0 + gate * (1.0 - sigmoid)))
    keep(2, grad * (gate * sigmoid))
    for s in range(last):
        chunks(3, s, terms_grad)
        rs_pair(1, s)
        if s < 2:
            rs_second(0, s)
        if s >= 2 and s - 2 < behind:
            rs_far(1, s - 2)
    rs_second(0, 2)
    rs_second(0, 3)
    for s in range(2, behind):
        rs_far(1, s)
    for s in range(min(2, behind)):
        rs_near(1, s)
    back_spread(2)
    back_spread(1)
    back_spread(3)
    over(0, CHUNKS // 2, weights_down)
    for s in range(min(2, behind)):
        rs_second(1, s)
    back_spread(0)
    for s in range(2, behind):
        rs_near(1, s)
    for s in range(behind, last):
        back_far(s)
    for s in range(SPLITS[2]):
        rs_last(0, s)
    for s in range(2, behind):
        rs_second(1, s)
    over(CHUNKS // 2, CHUNKS // 2, weights_down)
    for s in range(behind):
        rs_last(1, s)
    for s in range(behind, last):
        back_near(s)
    for s in range(behind, last):
        back_second(s)
    over(0, CHUNKS, weights_in)
    for s in range(SPLITS[2]):
        combine(0, s)
    for s in range(behind, last - 1):
        back_last(s)
    for s in range(behind):
        combine(1, s)

    def sent(ref, sem):
        remote(ref, ref, sem, sem, t, e).wait_send()

    ahead = AHEAD * (dim // SPLITS[0])
    sent(x.at[0, pl.ds(0, 7), :, :, pl.ds(ahead, dim - ahead)], ag_send.at[0])
    sent(x.at[1, pl.ds(0, 7)], ag_send.at[1])
    sent(x.at[0, pl.ds(0, 4), :, :, pl.ds(0, ahead)], mate_send)
    sent(ring.at[:, pl.ds(0, 3)], ring_send)
    sent(ringland.at[:, :, pl.ds(0, experts - 1)], spread_send)
    wait_cols = behind * (dim // last)
    sent(part.at[0, pl.ds(0, 7)], rs_send.at[0])
    sent(part.at[1, pl.ds(0, 7), :, :, pl.ds(0, wait_cols)], rs_send.at[1])
    sent(part.at[1, pl.ds(0, 4), :, :, pl.ds(wait_cols, dim - wait_cols)], backmate_send)
    sent(backslab.at[:, :, pl.ds(0, experts - 1)], back_send)
    sent(backslab.at[:, pl.ds(0, 3)], backring_send)
    for n, (first, end) in enumerate(
        ((AHEAD, SPLITS[0]), (0, SPLITS[1]), (0, SPLITS[2]), (0, behind))
    ):
        ref = slab[n].at[first:end, pl.ds(0, experts - 1)]
        sent(ref, a2a_send.at[n])
    back_last(last - 1)


def store(*refs):
    copies = [
        pltpu.make_async_copy(a, b, refs[-1].at[i])
        for i, (a, b) in enumerate(zip(refs[:4], refs[4:8]))
    ]
    for copy in copies:
        copy.start()
    for copy in copies:
        copy.wait()


def body(tokens, cotangent, expert_ids, gate_weights, w_in, w_down):
    experts = lax.axis_size("exp")
    rows, dim = tokens.shape
    ff = w_down.shape[1]
    group = CAP * PIECES
    hbm = pl.BlockSpec(memory_space=pltpu.HBM)
    vmem = pl.BlockSpec(memory_space=pltpu.VMEM)
    shape = jax.ShapeDtypeStruct
    dma = pltpu.SemaphoreType.DMA
    shapes = (tokens.shape, tokens.shape, w_in.shape, w_down.shape)
    boxes = [
        pltpu.VMEM((n, experts, group, dim // n // PIECES), BF16) for n in SPLITS
    ]
    results = pl.pallas_call(
        functools.partial(kernel, experts),
        out_shape=tuple(pltpu.VMEM(s, BF16) for s in shapes),
        in_specs=[hbm] * 6,
        out_specs=(vmem,) * 4,
        scratch_shapes=[
            pltpu.VMEM(expert_ids.shape[::-1], jnp.int32),
            pltpu.VMEM(expert_ids.shape[::-1], BF16),
            pltpu.VMEM((2, rows, dim), BF16),
            pltpu.VMEM((2, ff, dim), BF16),
            pltpu.VMEM((ff, dim), BF16),
            pltpu.VMEM((2, 8, 2, experts, dim), BF16),
            pltpu.VMEM((3, ff, 16 * experts), F32),
            pltpu.VMEM((3, ff, 16 * experts), BF16),
            pltpu.VMEM((16 * experts, ff), BF16),
            pltpu.VMEM((16 * experts, 2 * ff), BF16),
            pltpu.VMEM((2, 8, 2, experts, dim), BF16),
            pltpu.VMEM((2, 4, 2, experts, dim), BF16),
            pltpu.VMEM((2, 4, 2, experts, dim), BF16),
            pltpu.VMEM((2, 2, experts, dim), BF16),
            pltpu.VMEM((2, 2, 2, experts, dim), BF16),
            pltpu.VMEM((2, PIECES * rows, experts * group), BF16),
            dma((6,)),
            dma((4,)),
            dma((len(A2A),)),
            dma((2,)),
            dma((len(GATHER),)),
            dma((2,)),
            dma((len(REDUCE),)),
            pltpu.VMEM((AHEAD, 4) + boxes[0].shape[1:], BF16),
            pltpu.VMEM((AHEAD, 4) + boxes[0].shape[1:], BF16),
            dma(()),
            dma((AHEAD, 3)),
            dma(()),
            dma((AHEAD, 4)),
            dma(()),
            pltpu.VMEM((BEHIND, 4) + boxes[3].shape[1:], BF16),
            pltpu.VMEM((BEHIND, 4) + boxes[3].shape[1:], BF16),
            pltpu.VMEM((BEHIND, 2, experts // 2) + boxes[3].shape[2:], BF16),
            pltpu.VMEM((BEHIND, 2) + boxes[3].shape[1:], BF16),
            dma(()),
            dma((BEHIND, 4)),
            dma(()),
            dma((BEHIND, 2)),
            dma(()),
        ]
        + boxes * 2,
        compiler_params=pltpu.CompilerParams(
            collective_id=0, has_side_effects=True, vmem_limit_bytes=VMEM_LIMIT
        ),
    )(expert_ids.T, gate_weights.T, tokens, cotangent, w_in, w_down)
    return pl.pallas_call(
        store,
        out_shape=tuple(shape(s, BF16) for s in shapes),
        in_specs=[vmem] * 4,
        out_specs=(hbm,) * 4,
        scratch_shapes=[dma((4,))],
        compiler_params=pltpu.CompilerParams(vmem_limit_bytes=1024 * 1024),
    )(*results)


def solution(mesh):
    placed = (
        P(("tok", "exp"), None),
        P(("tok", "exp"), None),
        P(("tok", "exp"), None),
        P(("tok", "exp"), None),
        P("exp", None, "tok", None),
        P("exp", "tok", None),
    )
    return jax.shard_map(
        body,
        mesh=mesh,
        in_specs=placed,
        out_specs=(
            P(("tok", "exp"), None),
            P(("tok", "exp"), None),
            P("exp", None, "tok", None),
            P("exp", "tok", None),
        ),
        check_vma=False,
    )
```

```python
import functools

import jax
import jax.numpy as jnp
from jax import lax
from jax.experimental import pallas as pl
from jax.experimental.pallas import tpu as pltpu
from jax.sharding import PartitionSpec as P

CAP = 2
PIECES = 8
BF16 = jnp.bfloat16
F32 = jnp.float32
VMEM_LIMIT = 61_270_000
AHEAD = 3
CHUNKS = 4
BEHIND = 2
SPLITS = (4, 4, 4, 4)
MESH = pl.DeviceIdType.MESH


def dot(a, b):
    return jnp.dot(a, b, preferred_element_type=F32)


def dot_nt(a, b):
    return lax.dot_general(a, b, (((1,), (1,)), ((), ())), preferred_element_type=F32)


def dot_tn(a, b):
    return lax.dot_general(a, b, (((0,), (0,)), ((), ())), preferred_element_type=F32)


def iota(shape, dim):
    return lax.broadcasted_iota(jnp.int32, shape, dim)


def numbered(keys):
    return {key: i for i, key in enumerate(keys)}


A2A = numbered(
    (n, s)
    for n in range(4)
    for s in range(AHEAD if n == 0 else 0, SPLITS[n] - (BEHIND if n == 3 else 0))
)
GATHER = numbered(
    (q, s, kind)
    for q in range(2)
    for s in range(SPLITS[q])
    for kind in range(3 if q == 0 and s < AHEAD else 0, 4)
)
REDUCE = numbered(
    (q, s, kind)
    for q in range(2)
    for s in range(SPLITS[2 + q])
    for kind in range(2 if q == 1 and s >= SPLITS[3] - BEHIND else 0, 4)
)


def kernel(
    experts,
    ids_hbm,
    gates_hbm,
    tok_hbm,
    cot_hbm,
    win_hbm,
    wdn_hbm,
    moe,
    late,
    placed,
    gin,
    gdn,
    ids_ref,
    gates_ref,
    src,
    win,
    wdn,
    x,
    act,
    hid,
    hid_rows,
    pair_rows,
    part,
    mate,
    summed,
    far,
    near,
    back,
    in_sem,
    a2a_send,
    a2a_recv,
    ag_send,
    ag_recv,
    rs_send,
    rs_recv,
    ring,
    ringland,
    ring_send,
    ring_recv,
    spread_send,
    spread_recv,
    mate_send,
    backslab,
    backland,
    backfar,
    backnear,
    back_send,
    back_recv,
    backring_send,
    backring_recv,
    backmate_send,
    *boxes,
):
    slab, land = boxes[:4], boxes[4:]
    rows, dim = tok_hbm.shape
    group = CAP * PIECES
    slots = CAP * experts
    msg_rows = experts * group
    all_rows = 8 * slots
    chunk = dim // CHUNKS
    ff = win.shape[1]

    t = lax.axis_index("tok")
    e = lax.axis_index("exp")
    up = lax.rem(t + 2, 8)
    opp = lax.rem(t + 4, 8)
    dn = lax.rem(t + 6, 8)
    mate_t = t + 1 - 2 * lax.rem(t, 2)
    y = t // 2

    side = 4 if experts == 16 else 1
    line = experts // side

    def steps(k):
        a, b = k // line, k % line
        return min(a, side - a) + min(b, line - b)

    peers = [
        lax.rem(e // line + k // line, side) * line + lax.rem(lax.rem(e, line) + k % line, line)
        for k in sorted(range(1, experts), key=steps, reverse=True)
    ]
    barrier = pltpu.get_barrier_semaphore()
    for peer in peers:
        pl.semaphore_signal(barrier, inc=1, device_id=(t, peer), device_id_type=MESH)
    for other in (up, dn, mate_t):
        pl.semaphore_signal(barrier, inc=1, device_id=(other, e), device_id_type=MESH)

    loads = [
        pltpu.make_async_copy(a, b, in_sem.at[i])
        for i, (a, b) in enumerate(
            (
                (ids_hbm, ids_ref),
                (gates_hbm, gates_ref),
                (tok_hbm, src.at[0]),
                (cot_hbm, src.at[1]),
                (win_hbm.at[0], win),
                (wdn_hbm.at[0], wdn),
            )
        )
    ]
    for copy in loads:
        copy.start()

    def remote(a, b, ssem, rsem, dev_t, dev_e):
        return pltpu.make_async_remote_copy(
            src_ref=a,
            dst_ref=b,
            send_sem=ssem,
            recv_sem=rsem,
            device_id=(dev_t, dev_e),
            device_id_type=MESH,
        )

    loads[0].wait()
    loads[1].wait()
    ids = ids_ref[...]
    gates = gates_ref[...].astype(F32)
    row_e = iota((msg_rows, rows), 0) // group
    hits = jnp.zeros((msg_rows, rows), F32)
    weights = jnp.zeros((msg_rows, rows), F32)
    for k in range(ids.shape[0]):
        same = ids[k : k + 1, :] == row_e
        hits = hits + jnp.where(same, 1.0, 0.0)
        weights = weights + jnp.where(same, gates[k : k + 1, :], 0.0)
    earlier = jnp.where(iota((rows, rows), 0) < iota((rows, rows), 1), 1.0, 0.0)
    before = dot(hits.astype(BF16), earlier.astype(BF16))
    slot_of_row = lax.rem(iota((msg_rows, rows), 0), CAP).astype(F32)
    here = before == slot_of_row
    picked = jnp.where(here, hits, 0.0).astype(BF16)
    weighted = jnp.where(here, weights, 0.0).astype(BF16)
    wide = (msg_rows, PIECES * rows)
    tall = wide[::-1]

    def ones_where(test):
        return jnp.where(test, 1.0, 0.0).astype(BF16)

    def table(values):
        spread = ones_where(
            iota((rows, wide[1]), 0) == lax.rem(iota((rows, wide[1]), 1), rows)
        )
        same = lax.rem(iota(wide, 0), group) // CAP == iota(wide, 1) // rows
        return jnp.where(same, dot(values, spread), 0.0).astype(BF16)

    def back_table(values):
        spread = ones_where(
            lax.rem(iota((wide[1], rows), 0), rows) == iota((wide[1], rows), 1)
        )
        same = lax.rem(iota(tall, 1), group) // CAP == iota(tall, 0) // rows
        return jnp.where(same, dot_nt(spread, values), 0.0).astype(BF16)

    def span(n, s):
        size = dim // SPLITS[n]
        return pl.ds(s * size, size), size // PIECES

    def fill(n, s, placed):
        start, width = span(n, s)[0].start, span(n, s)[1]
        pieces = jnp.concatenate(
            [src[n, :, start + j * width : start + (j + 1) * width] for j in range(PIECES)],
            axis=0,
        )
        message = dot(placed, pieces).astype(BF16).reshape(experts, group, width)
        if n == 0 and s < AHEAD:
            ring[s, y] = message
        else:
            slab[n][s] = message

    def exchange(n, s):
        copies = [
            remote(
                slab[n].at[s, peer],
                land[n].at[s, e],
                a2a_send.at[n],
                a2a_recv.at[A2A[n, s]],
                t,
                peer,
            )
            for peer in peers
        ]
        for copy in copies:
            copy.start()
        land[n][s, e] = slab[n][s, e]

    def exchanged(n, s):
        ref = land[n].at[s, pl.ds(0, experts - 1)]
        remote(ref, ref, a2a_send.at[n], a2a_recv.at[A2A[n, s]], t, e).wait_recv()
        return land[n][s].reshape(msg_rows, span(n, s)[1])

    def ring_copy(s, n):
        d, half, dev = (
            (0, 0, up),
            (0, 1, up),
            (3, 0, up),
            (0, 1, dn),
            (0, 0, dn),
            (1, 1, dn),
        )[n]
        count = experts // 2
        ref = ring.at[s, lax.rem(y + d, 4), pl.ds(half * count, count)]
        return remote(ref, ref, ring_send, ring_recv.at[s, n % 3], dev, e)

    def ring_arrived(s, kind):
        ref = ring.at[s, 0]
        remote(ref, ref, ring_send, ring_recv.at[s, kind], t, e).wait_recv()

    def ring_first():
        for pair in ((0, 3), (1, 4)):
            for s in range(AHEAD):
                for n in pair:
                    ring_copy(s, n).start()

    def spread(s, d):
        block = lax.rem(y + d, 4)
        copies = [
            remote(
                ring.at[s, block, peer],
                ringland.at[s, d, e],
                spread_send,
                spread_recv.at[s, d],
                t,
                peer,
            )
            for peer in peers
        ]
        for copy in copies:
            copy.start()
        ringland[s, d, e] = ring[s, block, e]

    def ring_relay(s):
        ring_arrived(s, 0)
        for n in (2, 5):
            ring_copy(s, n).start()

    def ring_near(s):
        ring_arrived(s, 1)
        spread(s, 1)
        spread(s, 3)

    def ring_last(s):
        ring_arrived(s, 2)
        spread(s, 2)

    def ring_take(s, d):
        ref = ringland.at[s, d, pl.ds(0, experts - 1)]
        remote(ref, ref, spread_send, spread_recv.at[s, d], t, e).wait_recv()
        block = lax.rem(t + 2 * d, 8)
        put_rows(0, s, block, ringland[s, d])
        ref = x.at[0, block, :, :, span(0, s)[0]]
        remote(ref, ref, mate_send, ag_recv.at[GATHER[0, s, 3]], mate_t, e).start()

    pick_table = table(picked)
    loads[2].wait()
    for s in range(SPLITS[0]):
        fill(0, s, pick_table)
    pl.semaphore_wait(barrier, experts + 2)
    ring_first()
    for s in range(AHEAD, SPLITS[0]):
        exchange(0, s)
    weight_table = table(weighted)
    loads[3].wait()
    for s in range(SPLITS[1]):
        fill(1, s, weight_table)
    for s in range(SPLITS[1]):
        exchange(1, s)
    for s in range(AHEAD):
        spread(s, 0)

    square = (msg_rows, msg_rows)
    r0, r1 = iota(square, 0), iota(square, 1)
    gathers = ones_where(
        r1 == lax.rem(r0, slots) // CAP * group + r0 // slots * CAP + lax.rem(r0, CAP)
    )
    scatters = ones_where(
        r1 == lax.rem(r0, group) // CAP * slots + r0 // group * CAP + lax.rem(r0, CAP)
    )

    def put_rows(q, s, block, message):
        start, width = span(q, s)[0].start, span(q, s)[1]
        own = dot(gathers, message.reshape(msg_rows, width)).astype(BF16)
        own = own.reshape(PIECES, 2, experts, width)
        for j in range(PIECES):
            x[q, block, :, :, start + j * width : start + (j + 1) * width] = own[j]

    def take_rows(q, s):
        put_rows(q, s, t, exchanged(q, s))

    def ag_ref(q, s, block, half):
        cols = span(q, s)[0]
        if half is None:
            return x.at[q, block, :, :, cols]
        return x.at[q, block, half, :, cols]

    def ag(q, s, n):
        block, half, dev = (
            (t, 0, up),
            (t, 1, up),
            (dn, 0, up),
            (t, 1, dn),
            (t, 0, dn),
            (up, 1, dn),
            (t, None, mate_t),
            (dn, 0, mate_t),
            (up, 1, mate_t),
            (dn, 1, mate_t),
            (up, 0, mate_t),
            (opp, 0, mate_t),
            (opp, 1, mate_t),
        )[n]
        ref = ag_ref(q, s, block, half)
        return remote(ref, ref, ag_send.at[q], ag_recv.at[GATHER[q, s, n % 3 if n < 6 else 3]], dev, e)

    def ag_arrived(q, s, n):
        ref = x.at[q, pl.ds(0, 4 if n == 3 else 1), :, :, span(q, s)[0]]
        remote(ref, ref, ag_send.at[q], ag_recv.at[GATHER[q, s, n]], t, e).wait_recv()

    def ag_first(q, s):
        for n in (0, 3, 1, 4, 6):
            ag(q, s, n).start()

    def ag_relay(q, s):
        ag_arrived(q, s, 0)
        for n in (2, 5, 7, 8):
            ag(q, s, n).start()

    def ag_second(q, s):
        ag_arrived(q, s, 1)
        for n in (9, 10):
            ag(q, s, n).start()

    def ag_third(q, s):
        ag_arrived(q, s, 2)
        for n in (11, 12):
            ag(q, s, n).start()

    def ag_last(q, s):
        ag_arrived(q, s, 3)

    last = SPLITS[3]
    behind = last - BEHIND

    def rs(q, s, n):
        cols = span(2 + q, s)[0]
        if n >= 6:
            d = (2, 1, 3, 0)[n - 6]
            a = part.at[q, lax.rem(mate_t + 2 * d, 8), :, :, cols]
            b, dev = mate.at[q, d, :, :, cols], mate_t
        else:
            a, b, dev = (
                (summed.at[q, 2, 0, :, cols], far.at[q, 0, :, cols], up),
                (summed.at[q, 1, 1, :, cols], near.at[q, 0, 1, :, cols], up),
                (summed.at[q, 1, 0, :, cols], near.at[q, 0, 0, :, cols], up),
                (summed.at[q, 2, 1, :, cols], far.at[q, 1, :, cols], dn),
                (summed.at[q, 3, 0, :, cols], near.at[q, 1, 0, :, cols], dn),
                (summed.at[q, 3, 1, :, cols], near.at[q, 1, 1, :, cols], dn),
            )[n]
        kind = (0, 1, 1, 0, 1, 1, 2, 3, 3, 3)[n]
        sem = backmate_send if q == 1 and s >= behind else rs_send.at[q]
        return remote(a, b, sem, rs_recv.at[REDUCE[q, s, kind]], dev, e)

    def rs_arrived(q, s, kind):
        ref = (far.at[q], near.at[q], mate.at[q, 0], mate.at[q, pl.ds(0, 3)])[kind]
        ref = ref.at[..., span(2 + q, s)[0]]
        remote(ref, ref, rs_send.at[q], rs_recv.at[REDUCE[q, s, kind]], t, e).wait_recv()

    def rs_pair(q, s):
        for n in range(6, 10):
            rs(q, s, n).start()

    def chip_sum(q, s, d):
        cols = span(2 + q, s)[0]
        own = part[q, lax.rem(t + 2 * d, 8), :, :, cols].astype(F32)
        summed[q, d, :, :, cols] = (own + mate[q, d, :, :, cols].astype(F32)).astype(BF16)

    def rs_far(q, s):
        rs_arrived(q, s, 2)
        chip_sum(q, s, 2)
        rs(q, s, 0).start()
        rs(q, s, 3).start()

    def rs_near(q, s):
        rs_arrived(q, s, 3)
        chip_sum(q, s, 1)
        rs(q, s, 1).start()
        chip_sum(q, s, 3)
        rs(q, s, 4).start()

    def rs_second(q, s):
        cols = span(2 + q, s)[0]
        rs_arrived(q, s, 0)
        for way, d, half, n in ((0, 1, 0, 2), (1, 3, 1, 5)):
            total = summed[q, d, half, :, cols].astype(F32) + far[q, way, :, cols].astype(F32)
            summed[q, d, half, :, cols] = total.astype(BF16)
            rs(q, s, n).start()

    def as_message(total, width):
        total = total.astype(BF16).reshape(slots, PIECES * width)
        stacked = jnp.concatenate(
            [total[:, j * width : (j + 1) * width] for j in range(PIECES)], axis=0
        )
        return dot(scatters, stacked).astype(BF16).reshape(experts, group, width)

    def back_spread(d):
        for s in range(behind, last):
            cols, width = span(3, s)
            b = s - behind
            if d != 3 and d != 0:
                rs_arrived(1, s, 2 if d == 2 else 3)
            own = part[1, lax.rem(t + 2 * d, 8), :, :, cols].astype(F32)
            backslab[b, d] = as_message(own + mate[1, d, :, :, cols].astype(F32), width)
            copies = [
                remote(
                    backslab.at[b, d, peer],
                    backland.at[b, d, e],
                    back_send,
                    back_recv.at[b, d],
                    t,
                    peer,
                )
                for peer in peers
            ]
            for copy in copies:
                copy.start()
            backland[b, d, e] = backslab[b, d, e]

    def back_arrived(s, d):
        ref = backland.at[s - behind, d, pl.ds(0, experts - 1)]
        remote(ref, ref, back_send, back_recv.at[s - behind, d], t, e).wait_recv()

    low, high = pl.ds(0, experts // 2), pl.ds(experts // 2, experts // 2)

    def back_ring(s, d, half, ref, kind, dev):
        remote(
            backland.at[s - behind, d, half],
            ref,
            backring_send,
            backring_recv.at[s - behind, kind],
            dev,
            e,
        ).start()

    def back_ring_arrived(s, kind):
        ref = backnear.at[s - behind] if kind else backland.at[s - behind, 0]
        remote(ref, ref, backring_send, backring_recv.at[s - behind, kind], t, e).wait_recv()

    def back_far(s):
        b = s - behind
        back_arrived(s, 2)
        back_ring(s, 2, low, backfar.at[b, 0], 0, up)
        back_ring(s, 2, high, backfar.at[b, 1], 0, dn)

    def back_near(s):
        b = s - behind
        back_arrived(s, 1)
        back_ring(s, 1, high, backnear.at[b, 0, high], 1, up)
        back_arrived(s, 3)
        back_ring(s, 3, low, backnear.at[b, 1, low], 1, dn)

    def back_second(s):
        b = s - behind
        back_ring_arrived(s, 0)
        for way, d, half, dev in ((0, 1, low, up), (1, 3, high, dn)):
            total = backland[b, d, half].astype(F32) + backfar[b, way].astype(F32)
            backland[b, d, half] = total.astype(BF16)
            back_ring(s, d, half, backnear.at[b, way, half], 1, dev)

    def back_last(s):
        b = s - behind
        back_arrived(s, 0)
        own = backland[b, 0].astype(F32)
        back_ring_arrived(s, 1)
        total = own + backnear[b, 0].astype(F32) + backnear[b, 1].astype(F32)
        late[s] = total.astype(BF16).reshape(msg_rows, span(3, s)[1])

    def rs_last(q, s):
        cols, width = span(2 + q, s)
        total = part[q, t, :, :, cols].astype(F32) + mate[q, 0, :, :, cols].astype(F32)
        rs_arrived(q, s, 1)
        total = total + near[q, 0, :, :, cols].astype(F32) + near[q, 1, :, :, cols].astype(F32)
        slab[2 + q][s] = as_message(total, width)
        exchange(2 + q, s)

    def combine(s):
        put_back(moe, s, span(2, s), dot(back[...], exchanged(2, s)))

    def over(first, count, step):
        def body(k, carry):
            step(pl.ds(pl.multiple_of(k * chunk, chunk), chunk))
            return carry

        if count == 1:
            step(pl.ds(first * chunk, chunk))
        else:
            lax.fori_loop(first, first + count, body, 0)

    def chunks(n, s, step):
        count = CHUNKS // SPLITS[n]
        over(s * count, count, step)

    def forward(cols):
        piece = x[0, :, :, :, cols].reshape(all_rows, chunk)
        both = dot_nt(win[:, :, cols].reshape(2 * ff, chunk), piece)
        act[0:2] += both.reshape(2, ff, all_rows)

    def terms_out(cols):
        piece = dot(hid_rows[...], wdn[:, cols]).astype(BF16)
        part[0, :, :, :, cols] = piece.reshape(8, 2, experts, chunk)

    def backward(cols):
        piece = x[1, :, :, :, cols].reshape(all_rows, chunk)
        act[2] += dot_nt(wdn[:, cols], piece)

    def terms_grad(cols):
        piece = dot(pair_rows[...], win[:, :, cols].reshape(2 * ff, chunk))
        part[1, :, :, :, cols] = piece.astype(BF16).reshape(8, 2, experts, chunk)

    def weights_down(cols):
        piece = x[1, :, :, :, cols].reshape(all_rows, chunk)
        gdn[0, :, cols] = dot(hid[0], piece).astype(BF16)

    def weights_in(cols):
        piece = x[0, :, :, :, cols].reshape(all_rows, chunk)
        both = dot(hid[1:3].reshape(2 * ff, all_rows), piece).astype(BF16)
        gin[0, :, :, cols] = both.reshape(2, ff, chunk)

    def keep(i, value):
        hid[i] = value.astype(BF16)
        if i == 0:
            hid_rows[...] = value.T.astype(BF16)
        else:
            pair_rows[:, (i - 1) * ff : i * ff] = value.T.astype(BF16)

    act[...] = jnp.zeros_like(act)
    for s in range(AHEAD):
        ring_relay(s)
    later = range(AHEAD, SPLITS[0])
    for s in later:
        take_rows(0, s)
        ag_first(0, s)
    for s in range(AHEAD):
        ring_near(s)
    for s in range(SPLITS[1]):
        take_rows(1, s)
    for s in later:
        ag_relay(0, s)
        if s == AHEAD:
            for a in range(AHEAD):
                ring_last(a)
    for s in range(SPLITS[1]):
        ag_first(1, s)
    for s in range(AHEAD):
        ring_take(s, 0)
    for s in later:
        ag_second(0, s)
    placed[...] = back_table(picked)
    back[...] = back_table(weighted)
    for s in later:
        ag_third(0, s)
    for s in range(AHEAD):
        ring_take(s, 1)
        ring_take(s, 3)
    loads[4].wait()
    loads[5].wait()
    for s in later:
        ag_last(0, s)
        chunks(0, s, forward)
    ag_relay(1, 0)
    for s in range(AHEAD):
        ring_take(s, 2)
    ag_relay(1, 1)
    for s in range(AHEAD):
        ag_last(0, s)
        chunks(0, s, forward)
    ag_relay(1, 2)

    gate = act[0]
    keep(0, gate * jax.nn.sigmoid(gate) * act[1])
    for s in range(SPLITS[2]):
        chunks(2, s, terms_out)
        rs_pair(0, s)
        if s == 1:
            ag_relay(1, 3)
        if s >= 2:
            rs_far(0, s - 2)
    for s in range(SPLITS[1]):
        ag_second(1, s)
    rs_far(0, 2)
    rs_far(0, 3)
    rs_near(0, 0)
    rs_near(0, 1)
    ag_third(1, 0)
    ag_third(1, 1)
    rs_near(0, 2)
    rs_near(0, 3)
    for s in range(SPLITS[1]):
        if s < 2:
            ag_third(1, s + 2)
        ag_last(1, s)
        chunks(1, s, backward)

    gate = act[0]
    sigmoid = jax.nn.sigmoid(gate)
    grad = act[2]
    keep(1, grad * act[1] * sigmoid * (1.0 + gate * (1.0 - sigmoid)))
    keep(2, grad * (gate * sigmoid))
    for s in range(last):
        chunks(3, s, terms_grad)
        rs_pair(1, s)
        if s < 2:
            rs_second(0, s)
        if s >= 2 and s - 2 < behind:
            rs_far(1, s - 2)
    rs_second(0, 2)
    rs_second(0, 3)
    for s in range(2, behind):
        rs_far(1, s)
    for s in range(min(2, behind)):
        rs_near(1, s)
    back_spread(2)
    back_spread(1)
    back_spread(3)
    over(0, CHUNKS // 2, weights_down)
    for s in range(min(2, behind)):
        rs_second(1, s)
    back_spread(0)
    for s in range(2, behind):
        rs_near(1, s)
    for s in range(behind, last):
        back_far(s)
    for s in range(SPLITS[2]):
        rs_last(0, s)
    for s in range(2, behind):
        rs_second(1, s)
    over(CHUNKS // 2, CHUNKS // 2, weights_down)
    for s in range(behind):
        rs_last(1, s)
    for s in range(behind, last):
        back_near(s)
    for s in range(behind, last):
        back_second(s)
    over(0, CHUNKS, weights_in)
    for s in range(SPLITS[2]):
        combine(s)
    for s in range(behind, last - 1):
        back_last(s)
    for s in range(behind):
        late[s] = exchanged(3, s)

    def sent(ref, sem):
        remote(ref, ref, sem, sem, t, e).wait_send()

    ahead = AHEAD * (dim // SPLITS[0])
    sent(x.at[0, pl.ds(0, 7), :, :, pl.ds(ahead, dim - ahead)], ag_send.at[0])
    sent(x.at[1, pl.ds(0, 7)], ag_send.at[1])
    sent(x.at[0, pl.ds(0, 4), :, :, pl.ds(0, ahead)], mate_send)
    sent(ring.at[:, pl.ds(0, 3)], ring_send)
    sent(ringland.at[:, :, pl.ds(0, experts - 1)], spread_send)
    wait_cols = behind * (dim // last)
    sent(part.at[0, pl.ds(0, 7)], rs_send.at[0])
    sent(part.at[1, pl.ds(0, 7), :, :, pl.ds(0, wait_cols)], rs_send.at[1])
    sent(part.at[1, pl.ds(0, 4), :, :, pl.ds(wait_cols, dim - wait_cols)], backmate_send)
    sent(backslab.at[:, :, pl.ds(0, experts - 1)], back_send)
    sent(backslab.at[:, pl.ds(0, 3)], backring_send)
    for n, (first, end) in enumerate(
        ((AHEAD, SPLITS[0]), (0, SPLITS[1]), (0, SPLITS[2]), (0, behind))
    ):
        ref = slab[n].at[first:end, pl.ds(0, experts - 1)]
        sent(ref, a2a_send.at[n])
    back_last(last - 1)


def put_back(out, s, cols, values):
    start, width = cols[0].start, cols[1]
    rows = out.shape[0]
    values = values.astype(BF16)
    for j in range(PIECES):
        out[:, start + j * width : start + (j + 1) * width] = values[j * rows : (j + 1) * rows]


def store(moe, late, placed, gin, gdn, moe_hbm, tgr_hbm, gin_hbm, gdn_hbm, tgr, sem):
    copies = [
        pltpu.make_async_copy(a, b, sem.at[i])
        for i, (a, b) in enumerate(((gin, gin_hbm), (gdn, gdn_hbm), (moe, moe_hbm)))
    ]
    for copy in copies:
        copy.start()
    count = late.shape[0]
    size = tgr.shape[1] // count
    for s in range(count):
        cols = pl.ds(s * size, size)
        put_back(tgr, s, (cols, size // PIECES), dot(placed[...], late[s]))
        copy = pltpu.make_async_copy(tgr.at[:, cols], tgr_hbm.at[:, cols], sem.at[3 + s])
        copy.start()
        copies.append(copy)
    for copy in copies:
        copy.wait()


def body(tokens, cotangent, expert_ids, gate_weights, w_in, w_down):
    experts = lax.axis_size("exp")
    rows, dim = tokens.shape
    ff = w_down.shape[1]
    group = CAP * PIECES
    hbm = pl.BlockSpec(memory_space=pltpu.HBM)
    vmem = pl.BlockSpec(memory_space=pltpu.VMEM)
    shape = jax.ShapeDtypeStruct
    dma = pltpu.SemaphoreType.DMA
    shapes = (tokens.shape, tokens.shape, w_in.shape, w_down.shape)
    boxes = [
        pltpu.VMEM((n, experts, group, dim // n // PIECES), BF16) for n in SPLITS
    ]
    kept = (
        tokens.shape,
        (SPLITS[3], experts * group, dim // SPLITS[3] // PIECES),
        (PIECES * rows, experts * group),
        w_in.shape,
        w_down.shape,
    )
    results = pl.pallas_call(
        functools.partial(kernel, experts),
        out_shape=tuple(pltpu.VMEM(s, BF16) for s in kept),
        in_specs=[hbm] * 6,
        out_specs=(vmem,) * 5,
        scratch_shapes=[
            pltpu.VMEM(expert_ids.shape[::-1], jnp.int32),
            pltpu.VMEM(expert_ids.shape[::-1], BF16),
            pltpu.VMEM((2, rows, dim), BF16),
            pltpu.VMEM((2, ff, dim), BF16),
            pltpu.VMEM((ff, dim), BF16),
            pltpu.VMEM((2, 8, 2, experts, dim), BF16),
            pltpu.VMEM((3, ff, 16 * experts), F32),
            pltpu.VMEM((3, ff, 16 * experts), BF16),
            pltpu.VMEM((16 * experts, ff), BF16),
            pltpu.VMEM((16 * experts, 2 * ff), BF16),
            pltpu.VMEM((2, 8, 2, experts, dim), BF16),
            pltpu.VMEM((2, 4, 2, experts, dim), BF16),
            pltpu.VMEM((2, 4, 2, experts, dim), BF16),
            pltpu.VMEM((2, 2, experts, dim), BF16),
            pltpu.VMEM((2, 2, 2, experts, dim), BF16),
            pltpu.VMEM((PIECES * rows, experts * group), BF16),
            dma((6,)),
            dma((4,)),
            dma((len(A2A),)),
            dma((2,)),
            dma((len(GATHER),)),
            dma((2,)),
            dma((len(REDUCE),)),
            pltpu.VMEM((AHEAD, 4) + boxes[0].shape[1:], BF16),
            pltpu.VMEM((AHEAD, 4) + boxes[0].shape[1:], BF16),
            dma(()),
            dma((AHEAD, 3)),
            dma(()),
            dma((AHEAD, 4)),
            dma(()),
            pltpu.VMEM((BEHIND, 4) + boxes[3].shape[1:], BF16),
            pltpu.VMEM((BEHIND, 4) + boxes[3].shape[1:], BF16),
            pltpu.VMEM((BEHIND, 2, experts // 2) + boxes[3].shape[2:], BF16),
            pltpu.VMEM((BEHIND, 2) + boxes[3].shape[1:], BF16),
            dma(()),
            dma((BEHIND, 4)),
            dma(()),
            dma((BEHIND, 2)),
            dma(()),
        ]
        + boxes * 2,
        compiler_params=pltpu.CompilerParams(
            collective_id=0, has_side_effects=True, vmem_limit_bytes=VMEM_LIMIT
        ),
    )(expert_ids.T, gate_weights.T, tokens, cotangent, w_in, w_down)
    return pl.pallas_call(
        store,
        out_shape=tuple(shape(s, BF16) for s in shapes),
        in_specs=[vmem] * 5,
        out_specs=(hbm,) * 4,
        scratch_shapes=[pltpu.VMEM(tokens.shape, BF16), dma((3 + SPLITS[3],))],
        compiler_params=pltpu.CompilerParams(vmem_limit_bytes=4 * 1024 * 1024),
    )(*results)


def solution(mesh):
    placed = (
        P(("tok", "exp"), None),
        P(("tok", "exp"), None),
        P(("tok", "exp"), None),
        P(("tok", "exp"), None),
        P("exp", None, "tok", None),
        P("exp", "tok", None),
    )
    return jax.shard_map(
        body,
        mesh=mesh,
        in_specs=placed,
        out_specs=(
            P(("tok", "exp"), None),
            P(("tok", "exp"), None),
            P("exp", None, "tok", None),
            P("exp", "tok", None),
        ),
        check_vma=False,
    )
```

```python
import functools

import jax
import jax.numpy as jnp
from jax import lax
from jax.experimental import pallas as pl
from jax.experimental.pallas import tpu as pltpu
from jax.sharding import PartitionSpec as P

CAP = 2
PIECES = 8
BF16 = jnp.bfloat16
F32 = jnp.float32
VMEM_LIMIT = 61_270_000
AHEAD = 3
CHUNKS = 4
BEHIND = 2
SPLITS = (4, 4, 4, 4)
MESH = pl.DeviceIdType.MESH


def dot(a, b):
    return jnp.dot(a, b, preferred_element_type=F32)


def dot_nt(a, b):
    return lax.dot_general(a, b, (((1,), (1,)), ((), ())), preferred_element_type=F32)


def dot_tn(a, b):
    return lax.dot_general(a, b, (((0,), (0,)), ((), ())), preferred_element_type=F32)


def iota(shape, dim):
    return lax.broadcasted_iota(jnp.int32, shape, dim)


def numbered(keys):
    return {key: i for i, key in enumerate(keys)}


A2A = numbered(
    (n, s)
    for n in range(4)
    for s in range(AHEAD if n == 0 else 0, SPLITS[n] - (BEHIND if n == 3 else 0))
)
GATHER = numbered(
    (q, s, kind)
    for q in range(2)
    for s in range(SPLITS[q])
    for kind in range(3 if q == 0 and s < AHEAD else 0, 4)
)
REDUCE = numbered(
    (q, s, kind)
    for q in range(2)
    for s in range(SPLITS[2 + q])
    for kind in range(2 if q == 1 and s >= SPLITS[3] - BEHIND else 0, 4)
)


def kernel(
    experts,
    ids_hbm,
    gates_hbm,
    tok_hbm,
    cot_hbm,
    win_hbm,
    wdn_hbm,
    moe,
    late,
    placed,
    gin,
    gdn,
    ids_ref,
    gates_ref,
    src,
    win,
    wdn,
    x,
    act,
    hid,
    hid_rows,
    pair_rows,
    part,
    mate,
    summed,
    far,
    near,
    back,
    in_sem,
    a2a_send,
    a2a_recv,
    ag_send,
    ag_recv,
    rs_send,
    rs_recv,
    ring,
    ringland,
    ring_send,
    ring_recv,
    spread_send,
    spread_recv,
    mate_send,
    backslab,
    backland,
    backfar,
    backnear,
    back_send,
    back_recv,
    backring_send,
    backring_recv,
    backmate_send,
    *boxes,
):
    slab, land = boxes[:4], boxes[4:]
    rows, dim = tok_hbm.shape
    group = CAP * PIECES
    slots = CAP * experts
    msg_rows = experts * group
    all_rows = 8 * slots
    chunk = dim // CHUNKS
    ff = win.shape[1]

    t = lax.axis_index("tok")
    e = lax.axis_index("exp")
    up = lax.rem(t + 2, 8)
    opp = lax.rem(t + 4, 8)
    dn = lax.rem(t + 6, 8)
    mate_t = t + 1 - 2 * lax.rem(t, 2)
    y = t // 2

    side = 4 if experts == 16 else 1
    line = experts // side

    def steps(k):
        a, b = k // line, k % line
        return min(a, side - a) + min(b, line - b)

    peers = [
        lax.rem(e // line + k // line, side) * line + lax.rem(lax.rem(e, line) + k % line, line)
        for k in sorted(range(1, experts), key=steps, reverse=True)
    ]
    barrier = pltpu.get_barrier_semaphore()
    for peer in peers:
        pl.semaphore_signal(barrier, inc=1, device_id=(t, peer), device_id_type=MESH)
    for other in (up, dn, mate_t):
        pl.semaphore_signal(barrier, inc=1, device_id=(other, e), device_id_type=MESH)

    loads = [
        pltpu.make_async_copy(a, b, in_sem.at[i])
        for i, (a, b) in enumerate(
            (
                (ids_hbm, ids_ref),
                (gates_hbm, gates_ref),
                (tok_hbm, src.at[0]),
                (cot_hbm, src.at[1]),
                (win_hbm.at[0], win),
                (wdn_hbm.at[0], wdn),
            )
        )
    ]
    for copy in loads:
        copy.start()

    def remote(a, b, ssem, rsem, dev_t, dev_e):
        return pltpu.make_async_remote_copy(
            src_ref=a,
            dst_ref=b,
            send_sem=ssem,
            recv_sem=rsem,
            device_id=(dev_t, dev_e),
            device_id_type=MESH,
        )

    loads[0].wait()
    loads[1].wait()
    ids = ids_ref[...]
    gates = gates_ref[...].astype(F32)
    row_e = iota((msg_rows, rows), 0) // group
    hits = jnp.zeros((msg_rows, rows), F32)
    weights = jnp.zeros((msg_rows, rows), F32)
    for k in range(ids.shape[0]):
        same = ids[k : k + 1, :] == row_e
        hits = hits + jnp.where(same, 1.0, 0.0)
        weights = weights + jnp.where(same, gates[k : k + 1, :], 0.0)
    earlier = jnp.where(iota((rows, rows), 0) < iota((rows, rows), 1), 1.0, 0.0)
    before = dot(hits.astype(BF16), earlier.astype(BF16))
    slot_of_row = lax.rem(iota((msg_rows, rows), 0), CAP).astype(F32)
    here = before == slot_of_row
    picked = jnp.where(here, hits, 0.0).astype(BF16)
    weighted = jnp.where(here, weights, 0.0).astype(BF16)
    wide = (msg_rows, PIECES * rows)
    tall = wide[::-1]

    def ones_where(test):
        return jnp.where(test, 1.0, 0.0).astype(BF16)

    def table(values):
        spread = ones_where(
            iota((rows, wide[1]), 0) == lax.rem(iota((rows, wide[1]), 1), rows)
        )
        same = lax.rem(iota(wide, 0), group) // CAP == iota(wide, 1) // rows
        return jnp.where(same, dot(values, spread), 0.0).astype(BF16)

    def back_table(values):
        spread = ones_where(
            lax.rem(iota((wide[1], rows), 0), rows) == iota((wide[1], rows), 1)
        )
        same = lax.rem(iota(tall, 1), group) // CAP == iota(tall, 0) // rows
        return jnp.where(same, dot_nt(spread, values), 0.0).astype(BF16)

    def span(n, s):
        size = dim // SPLITS[n]
        return pl.ds(s * size, size), size // PIECES

    def fill(n, s, placed):
        start, width = span(n, s)[0].start, span(n, s)[1]
        pieces = jnp.concatenate(
            [src[n, :, start + j * width : start + (j + 1) * width] for j in range(PIECES)],
            axis=0,
        )
        message = dot(placed, pieces).astype(BF16).reshape(experts, group, width)
        if n == 0 and s < AHEAD:
            ring[s, y] = message
        else:
            slab[n][s] = message

    def exchange(n, s):
        copies = [
            remote(
                slab[n].at[s, peer],
                land[n].at[s, e],
                a2a_send.at[n],
                a2a_recv.at[A2A[n, s]],
                t,
                peer,
            )
            for peer in peers
        ]
        for copy in copies:
            copy.start()
        land[n][s, e] = slab[n][s, e]

    def exchanged(n, s):
        ref = land[n].at[s, pl.ds(0, experts - 1)]
        remote(ref, ref, a2a_send.at[n], a2a_recv.at[A2A[n, s]], t, e).wait_recv()
        return land[n][s].reshape(msg_rows, span(n, s)[1])

    def ring_copy(s, n):
        d, half, dev = (
            (0, 0, up),
            (0, 1, up),
            (3, 0, up),
            (0, 1, dn),
            (0, 0, dn),
            (1, 1, dn),
        )[n]
        count = experts // 2
        ref = ring.at[s, lax.rem(y + d, 4), pl.ds(half * count, count)]
        return remote(ref, ref, ring_send, ring_recv.at[s, n % 3], dev, e)

    def ring_arrived(s, kind):
        ref = ring.at[s, 0]
        remote(ref, ref, ring_send, ring_recv.at[s, kind], t, e).wait_recv()

    def ring_first():
        for pair in ((0, 3), (1, 4)):
            for s in range(AHEAD):
                for n in pair:
                    ring_copy(s, n).start()

    def spread(s, d):
        block = lax.rem(y + d, 4)
        copies = [
            remote(
                ring.at[s, block, peer],
                ringland.at[s, d, e],
                spread_send,
                spread_recv.at[s, d],
                t,
                peer,
            )
            for peer in peers
        ]
        for copy in copies:
            copy.start()
        ringland[s, d, e] = ring[s, block, e]

    def ring_relay(s):
        ring_arrived(s, 0)
        for n in (2, 5):
            ring_copy(s, n).start()

    def ring_near(s):
        ring_arrived(s, 1)
        spread(s, 1)
        spread(s, 3)

    def ring_last(s):
        ring_arrived(s, 2)
        spread(s, 2)

    def ring_take(s, d):
        ref = ringland.at[s, d, pl.ds(0, experts - 1)]
        remote(ref, ref, spread_send, spread_recv.at[s, d], t, e).wait_recv()
        block = lax.rem(t + 2 * d, 8)
        put_rows(0, s, block, ringland[s, d])
        ref = x.at[0, block, :, :, span(0, s)[0]]
        remote(ref, ref, mate_send, ag_recv.at[GATHER[0, s, 3]], mate_t, e).start()

    pick_table = table(picked)
    loads[2].wait()
    for s in range(SPLITS[0]):
        fill(0, s, pick_table)
    pl.semaphore_wait(barrier, experts + 2)
    ring_first()
    for s in range(AHEAD, SPLITS[0]):
        exchange(0, s)
    weight_table = table(weighted)
    loads[3].wait()
    for s in range(SPLITS[1]):
        fill(1, s, weight_table)
    for s in range(SPLITS[1]):
        exchange(1, s)
    for s in range(AHEAD):
        spread(s, 0)

    square = (msg_rows, msg_rows)
    r0, r1 = iota(square, 0), iota(square, 1)
    gathers = ones_where(
        r1 == lax.rem(r0, slots) // CAP * group + r0 // slots * CAP + lax.rem(r0, CAP)
    )
    scatters = ones_where(
        r1 == lax.rem(r0, group) // CAP * slots + r0 // group * CAP + lax.rem(r0, CAP)
    )

    def put_rows(q, s, block, message):
        start, width = span(q, s)[0].start, span(q, s)[1]
        own = dot(gathers, message.reshape(msg_rows, width)).astype(BF16)
        own = own.reshape(PIECES, 2, experts, width)
        for j in range(PIECES):
            x[q, block, :, :, start + j * width : start + (j + 1) * width] = own[j]

    def take_rows(q, s):
        put_rows(q, s, t, exchanged(q, s))

    def ag_ref(q, s, block, half):
        cols = span(q, s)[0]
        if half is None:
            return x.at[q, block, :, :, cols]
        return x.at[q, block, half, :, cols]

    def ag(q, s, n):
        block, half, dev = (
            (t, 0, up),
            (t, 1, up),
            (dn, 0, up),
            (t, 1, dn),
            (t, 0, dn),
            (up, 1, dn),
            (t, None, mate_t),
            (dn, 0, mate_t),
            (up, 1, mate_t),
            (dn, 1, mate_t),
            (up, 0, mate_t),
            (opp, 0, mate_t),
            (opp, 1, mate_t),
        )[n]
        ref = ag_ref(q, s, block, half)
        return remote(ref, ref, ag_send.at[q], ag_recv.at[GATHER[q, s, n % 3 if n < 6 else 3]], dev, e)

    def ag_arrived(q, s, n):
        ref = x.at[q, pl.ds(0, 4 if n == 3 else 1), :, :, span(q, s)[0]]
        remote(ref, ref, ag_send.at[q], ag_recv.at[GATHER[q, s, n]], t, e).wait_recv()

    def ag_first(q, s):
        for n in (0, 3, 1, 4, 6):
            ag(q, s, n).start()

    def ag_relay(q, s):
        ag_arrived(q, s, 0)
        for n in (2, 5, 7, 8):
            ag(q, s, n).start()

    def ag_second(q, s):
        ag_arrived(q, s, 1)
        for n in (9, 10):
            ag(q, s, n).start()

    def ag_third(q, s):
        ag_arrived(q, s, 2)
        for n in (11, 12):
            ag(q, s, n).start()

    def ag_last(q, s):
        ag_arrived(q, s, 3)

    last = SPLITS[3]
    behind = last - BEHIND

    def rs(q, s, n):
        cols = span(2 + q, s)[0]
        if n >= 6:
            d = (2, 1, 3, 0)[n - 6]
            a = part.at[q, lax.rem(mate_t + 2 * d, 8), :, :, cols]
            b, dev = mate.at[q, d, :, :, cols], mate_t
        else:
            a, b, dev = (
                (summed.at[q, 2, 0, :, cols], far.at[q, 0, :, cols], up),
                (summed.at[q, 1, 1, :, cols], near.at[q, 0, 1, :, cols], up),
                (summed.at[q, 1, 0, :, cols], near.at[q, 0, 0, :, cols], up),
                (summed.at[q, 2, 1, :, cols], far.at[q, 1, :, cols], dn),
                (summed.at[q, 3, 0, :, cols], near.at[q, 1, 0, :, cols], dn),
                (summed.at[q, 3, 1, :, cols], near.at[q, 1, 1, :, cols], dn),
            )[n]
        kind = (0, 1, 1, 0, 1, 1, 2, 3, 3, 3)[n]
        sem = backmate_send if q == 1 and s >= behind else rs_send.at[q]
        return remote(a, b, sem, rs_recv.at[REDUCE[q, s, kind]], dev, e)

    def rs_arrived(q, s, kind):
        ref = (far.at[q], near.at[q], mate.at[q, 0], mate.at[q, pl.ds(0, 3)])[kind]
        ref = ref.at[..., span(2 + q, s)[0]]
        remote(ref, ref, rs_send.at[q], rs_recv.at[REDUCE[q, s, kind]], t, e).wait_recv()

    def rs_pair(q, s):
        for n in range(6, 10):
            rs(q, s, n).start()

    def chip_sum(q, s, d):
        cols = span(2 + q, s)[0]
        own = part[q, lax.rem(t + 2 * d, 8), :, :, cols].astype(F32)
        summed[q, d, :, :, cols] = (own + mate[q, d, :, :, cols].astype(F32)).astype(BF16)

    def rs_far(q, s):
        rs_arrived(q, s, 2)
        chip_sum(q, s, 2)
        rs(q, s, 0).start()
        rs(q, s, 3).start()

    def rs_near(q, s):
        rs_arrived(q, s, 3)
        chip_sum(q, s, 1)
        rs(q, s, 1).start()
        chip_sum(q, s, 3)
        rs(q, s, 4).start()

    def rs_second(q, s):
        cols = span(2 + q, s)[0]
        rs_arrived(q, s, 0)
        for way, d, half, n in ((0, 1, 0, 2), (1, 3, 1, 5)):
            total = summed[q, d, half, :, cols].astype(F32) + far[q, way, :, cols].astype(F32)
            summed[q, d, half, :, cols] = total.astype(BF16)
            rs(q, s, n).start()

    def as_message(total, width):
        total = total.astype(BF16).reshape(slots, PIECES * width)
        stacked = jnp.concatenate(
            [total[:, j * width : (j + 1) * width] for j in range(PIECES)], axis=0
        )
        return dot(scatters, stacked).astype(BF16).reshape(experts, group, width)

    def back_spread(d):
        for s in range(behind, last):
            cols, width = span(3, s)
            b = s - behind
            if d != 3 and d != 0:
                rs_arrived(1, s, 2 if d == 2 else 3)
            own = part[1, lax.rem(t + 2 * d, 8), :, :, cols].astype(F32)
            backslab[b, d] = as_message(own + mate[1, d, :, :, cols].astype(F32), width)
            copies = [
                remote(
                    backslab.at[b, d, peer],
                    backland.at[b, d, e],
                    back_send,
                    back_recv.at[b, d],
                    t,
                    peer,
                )
                for peer in peers
            ]
            for copy in copies:
                copy.start()
            backland[b, d, e] = backslab[b, d, e]

    def back_arrived(s, d):
        ref = backland.at[s - behind, d, pl.ds(0, experts - 1)]
        remote(ref, ref, back_send, back_recv.at[s - behind, d], t, e).wait_recv()

    low, high = pl.ds(0, experts // 2), pl.ds(experts // 2, experts // 2)

    def back_ring(s, d, half, ref, kind, dev):
        remote(
            backland.at[s - behind, d, half],
            ref,
            backring_send,
            backring_recv.at[s - behind, kind],
            dev,
            e,
        ).start()

    def back_ring_arrived(s, kind):
        ref = backnear.at[s - behind] if kind else backland.at[s - behind, 0]
        remote(ref, ref, backring_send, backring_recv.at[s - behind, kind], t, e).wait_recv()

    def back_far(s):
        b = s - behind
        back_arrived(s, 2)
        back_ring(s, 2, low, backfar.at[b, 0], 0, up)
        back_ring(s, 2, high, backfar.at[b, 1], 0, dn)

    def back_near(s):
        b = s - behind
        back_arrived(s, 1)
        back_ring(s, 1, high, backnear.at[b, 0, high], 1, up)
        back_arrived(s, 3)
        back_ring(s, 3, low, backnear.at[b, 1, low], 1, dn)

    def back_second(s):
        b = s - behind
        back_ring_arrived(s, 0)
        for way, d, half, dev in ((0, 1, low, up), (1, 3, high, dn)):
            total = backland[b, d, half].astype(F32) + backfar[b, way].astype(F32)
            backland[b, d, half] = total.astype(BF16)
            back_ring(s, d, half, backnear.at[b, way, half], 1, dev)

    def back_last(s):
        b = s - behind
        back_arrived(s, 0)
        own = backland[b, 0].astype(F32)
        back_ring_arrived(s, 1)
        total = own + backnear[b, 0].astype(F32) + backnear[b, 1].astype(F32)
        late[s] = total.astype(BF16).reshape(msg_rows, span(3, s)[1])

    def rs_last(q, s):
        cols, width = span(2 + q, s)
        total = part[q, t, :, :, cols].astype(F32) + mate[q, 0, :, :, cols].astype(F32)
        rs_arrived(q, s, 1)
        total = total + near[q, 0, :, :, cols].astype(F32) + near[q, 1, :, :, cols].astype(F32)
        slab[2 + q][s] = as_message(total, width)
        exchange(2 + q, s)

    def combine(s):
        put_back(moe, s, span(2, s), dot(back[...], exchanged(2, s)))

    def over(first, count, step):
        def body(k, carry):
            step(pl.ds(pl.multiple_of(k * chunk, chunk), chunk))
            return carry

        if count == 1:
            step(pl.ds(first * chunk, chunk))
        else:
            lax.fori_loop(first, first + count, body, 0)

    def chunks(n, s, step):
        count = CHUNKS // SPLITS[n]
        over(s * count, count, step)

    def forward(cols):
        piece = x[0, :, :, :, cols].reshape(all_rows, chunk)
        both = dot_nt(win[:, :, cols].reshape(2 * ff, chunk), piece)
        act[0:2] += both.reshape(2, ff, all_rows)

    def terms_out(cols):
        piece = dot(hid_rows[...], wdn[:, cols]).astype(BF16)
        part[0, :, :, :, cols] = piece.reshape(8, 2, experts, chunk)

    def backward(cols):
        piece = x[1, :, :, :, cols].reshape(all_rows, chunk)
        act[2] += dot_nt(wdn[:, cols], piece)

    def terms_grad(cols):
        piece = dot(pair_rows[...], win[:, :, cols].reshape(2 * ff, chunk))
        part[1, :, :, :, cols] = piece.astype(BF16).reshape(8, 2, experts, chunk)

    def weights_down(cols):
        piece = x[1, :, :, :, cols].reshape(all_rows, chunk)
        gdn[0, :, cols] = dot(hid[0], piece).astype(BF16)

    def weights_in(cols):
        piece = x[0, :, :, :, cols].reshape(all_rows, chunk)
        both = dot(hid[1:3].reshape(2 * ff, all_rows), piece).astype(BF16)
        gin[0, :, :, cols] = both.reshape(2, ff, chunk)

    def keep(i, value):
        hid[i] = value.astype(BF16)
        if i == 0:
            hid_rows[...] = value.T.astype(BF16)
        else:
            pair_rows[:, (i - 1) * ff : i * ff] = value.T.astype(BF16)

    act[...] = jnp.zeros_like(act)
    for s in range(AHEAD):
        ring_relay(s)
    later = range(AHEAD, SPLITS[0])
    for s in later:
        take_rows(0, s)
        ag_first(0, s)
    for s in range(AHEAD):
        ring_near(s)
    for s in range(SPLITS[1]):
        take_rows(1, s)
    for s in later:
        ag_relay(0, s)
        if s == AHEAD:
            for a in range(AHEAD):
                ring_last(a)
    for s in range(SPLITS[1]):
        ag_first(1, s)
    for s in range(AHEAD):
        ring_take(s, 0)
    for s in later:
        ag_second(0, s)
    placed[...] = back_table(picked)
    back[...] = back_table(weighted)
    for s in range(AHEAD - 1):
        ring_take(s, 1)
        ring_take(s, 3)
    for s in later:
        ag_third(0, s)
    ring_take(AHEAD - 1, 1)
    ring_take(AHEAD - 1, 3)
    loads[4].wait()
    loads[5].wait()
    for s in later:
        ag_last(0, s)
        chunks(0, s, forward)
    ag_relay(1, 0)
    for s in range(AHEAD):
        ring_take(s, 2)
    ag_relay(1, 1)
    for s in range(AHEAD):
        ag_last(0, s)
        chunks(0, s, forward)
    ag_relay(1, 2)

    gate = act[0]
    keep(0, gate * jax.nn.sigmoid(gate) * act[1])
    for s in range(SPLITS[2]):
        chunks(2, s, terms_out)
        rs_pair(0, s)
        if s == 1:
            ag_relay(1, 3)
        if s >= 2:
            rs_far(0, s - 2)
    for s in range(SPLITS[1]):
        ag_second(1, s)
    rs_far(0, 2)
    rs_far(0, 3)
    rs_near(0, 0)
    rs_near(0, 1)
    ag_third(1, 0)
    ag_third(1, 1)
    rs_near(0, 2)
    rs_near(0, 3)
    for s in range(SPLITS[1]):
        if s < 2:
            ag_third(1, s + 2)
        ag_last(1, s)
        chunks(1, s, backward)

    gate = act[0]
    sigmoid = jax.nn.sigmoid(gate)
    grad = act[2]
    keep(1, grad * act[1] * sigmoid * (1.0 + gate * (1.0 - sigmoid)))
    keep(2, grad * (gate * sigmoid))
    for s in range(last):
        chunks(3, s, terms_grad)
        rs_pair(1, s)
        if s < 2:
            rs_second(0, s)
        if s >= 2 and s - 2 < behind:
            rs_far(1, s - 2)
    rs_second(0, 2)
    rs_second(0, 3)
    for s in range(2, behind):
        rs_far(1, s)
    for s in range(min(2, behind)):
        rs_near(1, s)
    back_spread(2)
    back_spread(1)
    back_spread(3)
    for s in range(min(2, behind)):
        rs_second(1, s)
    back_spread(0)
    for s in range(2, behind):
        rs_near(1, s)
    for s in range(behind, last):
        back_far(s)
    for s in range(SPLITS[2]):
        rs_last(0, s)
    for s in range(2, behind):
        rs_second(1, s)
    over(0, CHUNKS, weights_down)
    for s in range(behind):
        rs_last(1, s)
    for s in range(behind, last):
        back_near(s)
    for s in range(behind, last):
        back_second(s)
    over(0, CHUNKS, weights_in)
    for s in range(SPLITS[2]):
        combine(s)
    for s in range(behind, last - 1):
        back_last(s)
    for s in range(behind):
        late[s] = exchanged(3, s)

    def sent(ref, sem):
        remote(ref, ref, sem, sem, t, e).wait_send()

    ahead = AHEAD * (dim // SPLITS[0])
    sent(x.at[0, pl.ds(0, 7), :, :, pl.ds(ahead, dim - ahead)], ag_send.at[0])
    sent(x.at[1, pl.ds(0, 7)], ag_send.at[1])
    sent(x.at[0, pl.ds(0, 4), :, :, pl.ds(0, ahead)], mate_send)
    sent(ring.at[:, pl.ds(0, 3)], ring_send)
    sent(ringland.at[:, :, pl.ds(0, experts - 1)], spread_send)
    wait_cols = behind * (dim // last)
    sent(part.at[0, pl.ds(0, 7)], rs_send.at[0])
    sent(part.at[1, pl.ds(0, 7), :, :, pl.ds(0, wait_cols)], rs_send.at[1])
    sent(part.at[1, pl.ds(0, 4), :, :, pl.ds(wait_cols, dim - wait_cols)], backmate_send)
    sent(backslab.at[:, :, pl.ds(0, experts - 1)], back_send)
    sent(backslab.at[:, pl.ds(0, 3)], backring_send)
    for n, (first, end) in enumerate(
        ((AHEAD, SPLITS[0]), (0, SPLITS[1]), (0, SPLITS[2]), (0, behind))
    ):
        ref = slab[n].at[first:end, pl.ds(0, experts - 1)]
        sent(ref, a2a_send.at[n])
    back_last(last - 1)


def put_back(out, s, cols, values):
    start, width = cols[0].start, cols[1]
    rows = out.shape[0]
    values = values.astype(BF16)
    for j in range(PIECES):
        out[:, start + j * width : start + (j + 1) * width] = values[j * rows : (j + 1) * rows]


def store(moe, late, placed, gin, gdn, moe_hbm, tgr_hbm, gin_hbm, gdn_hbm, tgr, sem):
    copies = [
        pltpu.make_async_copy(a, b, sem.at[i])
        for i, (a, b) in enumerate(((gin, gin_hbm), (gdn, gdn_hbm), (moe, moe_hbm)))
    ]
    for copy in copies:
        copy.start()
    count = late.shape[0]
    size = tgr.shape[1] // count
    for s in range(count):
        cols = pl.ds(s * size, size)
        put_back(tgr, s, (cols, size // PIECES), dot(placed[...], late[s]))
        copy = pltpu.make_async_copy(tgr.at[:, cols], tgr_hbm.at[:, cols], sem.at[3 + s])
        copy.start()
        copies.append(copy)
    for copy in copies:
        copy.wait()


def body(tokens, cotangent, expert_ids, gate_weights, w_in, w_down):
    experts = lax.axis_size("exp")
    rows, dim = tokens.shape
    ff = w_down.shape[1]
    group = CAP * PIECES
    hbm = pl.BlockSpec(memory_space=pltpu.HBM)
    vmem = pl.BlockSpec(memory_space=pltpu.VMEM)
    shape = jax.ShapeDtypeStruct
    dma = pltpu.SemaphoreType.DMA
    shapes = (tokens.shape, tokens.shape, w_in.shape, w_down.shape)
    boxes = [
        pltpu.VMEM((n, experts, group, dim // n // PIECES), BF16) for n in SPLITS
    ]
    kept = (
        tokens.shape,
        (SPLITS[3], experts * group, dim // SPLITS[3] // PIECES),
        (PIECES * rows, experts * group),
        w_in.shape,
        w_down.shape,
    )
    results = pl.pallas_call(
        functools.partial(kernel, experts),
        out_shape=tuple(pltpu.VMEM(s, BF16) for s in kept),
        in_specs=[hbm] * 6,
        out_specs=(vmem,) * 5,
        scratch_shapes=[
            pltpu.VMEM(expert_ids.shape[::-1], jnp.int32),
            pltpu.VMEM(expert_ids.shape[::-1], BF16),
            pltpu.VMEM((2, rows, dim), BF16),
            pltpu.VMEM((2, ff, dim), BF16),
            pltpu.VMEM((ff, dim), BF16),
            pltpu.VMEM((2, 8, 2, experts, dim), BF16),
            pltpu.VMEM((3, ff, 16 * experts), F32),
            pltpu.VMEM((3, ff, 16 * experts), BF16),
            pltpu.VMEM((16 * experts, ff), BF16),
            pltpu.VMEM((16 * experts, 2 * ff), BF16),
            pltpu.VMEM((2, 8, 2, experts, dim), BF16),
            pltpu.VMEM((2, 4, 2, experts, dim), BF16),
            pltpu.VMEM((2, 4, 2, experts, dim), BF16),
            pltpu.VMEM((2, 2, experts, dim), BF16),
            pltpu.VMEM((2, 2, 2, experts, dim), BF16),
            pltpu.VMEM((PIECES * rows, experts * group), BF16),
            dma((6,)),
            dma((4,)),
            dma((len(A2A),)),
            dma((2,)),
            dma((len(GATHER),)),
            dma((2,)),
            dma((len(REDUCE),)),
            pltpu.VMEM((AHEAD, 4) + boxes[0].shape[1:], BF16),
            pltpu.VMEM((AHEAD, 4) + boxes[0].shape[1:], BF16),
            dma(()),
            dma((AHEAD, 3)),
            dma(()),
            dma((AHEAD, 4)),
            dma(()),
            pltpu.VMEM((BEHIND, 4) + boxes[3].shape[1:], BF16),
            pltpu.VMEM((BEHIND, 4) + boxes[3].shape[1:], BF16),
            pltpu.VMEM((BEHIND, 2, experts // 2) + boxes[3].shape[2:], BF16),
            pltpu.VMEM((BEHIND, 2) + boxes[3].shape[1:], BF16),
            dma(()),
            dma((BEHIND, 4)),
            dma(()),
            dma((BEHIND, 2)),
            dma(()),
        ]
        + boxes * 2,
        compiler_params=pltpu.CompilerParams(
            collective_id=0, has_side_effects=True, vmem_limit_bytes=VMEM_LIMIT
        ),
    )(expert_ids.T, gate_weights.T, tokens, cotangent, w_in, w_down)
    return pl.pallas_call(
        store,
        out_shape=tuple(shape(s, BF16) for s in shapes),
        in_specs=[vmem] * 5,
        out_specs=(hbm,) * 4,
        scratch_shapes=[pltpu.VMEM(tokens.shape, BF16), dma((3 + SPLITS[3],))],
        compiler_params=pltpu.CompilerParams(vmem_limit_bytes=4 * 1024 * 1024),
    )(*results)


def solution(mesh):
    placed = (
        P(("tok", "exp"), None),
        P(("tok", "exp"), None),
        P(("tok", "exp"), None),
        P(("tok", "exp"), None),
        P("exp", None, "tok", None),
        P("exp", "tok", None),
    )
    return jax.shard_map(
        body,
        mesh=mesh,
        in_specs=placed,
        out_specs=(
            P(("tok", "exp"), None),
            P(("tok", "exp"), None),
            P("exp", None, "tok", None),
            P("exp", "tok", None),
        ),
        check_vma=False,
    )
```
